256 devices in a mesh: band: 16 (over z, x_hi), fft: 16 (over x_lo, y, core).
Axes of the slice: x: 4 (x_hi: 2, x_lo: 2; x = x_hi * 2 + x_lo), y: 4, z: 8, core: 2. Of those that a mesh axis runs over, the one named last changes fastest.
Arguments:
- orbitals: bfloat16 [32, 128, 128, 128], P('band', 'fft'), may hold values from -6 to 6
- owner_order: int32 [2], replicated, may hold values from 0 to 15, as said below
- sphere_mask: int32 [128, 128, 128], P(None, 'fft'), may hold values from 0 to 1, as said below
Outputs:
- fock_images: float32 [32, 128, 128, 128], P('band', 'fft')
The draws below stay inside these ranges and needn't reach their ends.
Inputs may be any that keep to these rules, and one draw needn't show every extreme that they name: `owner_order`: the 2 owner groups are all different, and group 16 - 1 owns one of the rounds. `sphere_mask`: zero wherever q of the steps is less than the square of 56.
All inputs are finite; a program needn't handle non-finite values.
Results may differ from the reference program's by a relative error of at most 0.018.
Values may be sent and summed in bfloat16 or wider, within the bound.
A program may use at most 64 MiB of HBM per device.

```python
import jax
import jax.numpy as jnp
from jax import lax

GRID = 128
B_DEV = 2
ROUNDS = 2
GROUPS = 16
BANDS = 32


def draw_owner_order(key, part):
    shuffle_key = jax.random.fold_in(key, 11)
    slot_key = jax.random.fold_in(key, 23)
    shuffled = jax.random.permutation(shuffle_key, GROUPS).astype(jnp.int32)
    last_place = jnp.argmax(shuffled == GROUPS - 1).astype(jnp.int32)
    chosen_slot = jax.random.randint(slot_key, (), 0, ROUNDS).astype(jnp.int32)
    target = jnp.where(last_place < ROUNDS, last_place, chosen_slot).astype(jnp.int32)
    displaced = shuffled[target]
    shuffled = shuffled.at[last_place].set(displaced)
    shuffled = shuffled.at[target].set(jnp.int32(GROUPS - 1))
    return shuffled[:ROUNDS].astype(jnp.int32)


def draw_sphere_mask(key, part):
    bits_key = jax.random.fold_in(key, 37)
    shape = (GRID, GRID, GRID)
    random_bits = jax.random.randint(bits_key, shape, 0, 2).astype(jnp.int32)
    along_z = lax.broadcasted_iota(jnp.int32, shape, 0)
    along_y = lax.broadcasted_iota(jnp.int32, shape, 1)
    along_x = lax.broadcasted_iota(jnp.int32, shape, 2)

    def signed(values):
        return jnp.where(values < GRID // 2, values, values - GRID)
    freq_z, freq_y, freq_x = (signed(along_z), signed(along_y), signed(along_x))
    total_sq = freq_z * freq_z + freq_y * freq_y + freq_x * freq_x
    radius = 7 * GRID // 16
    return jnp.where(total_sq >= radius * radius, random_bits, jnp.int32(0)).astype(jnp.int32)


def shard_levels(stream_key, extent, shards, smallest, largest):
    loudness, own = 1.0, jax.random.fold_in(stream_key, 6)
    for dim, blocks in shards:
        steps = jnp.exp(jax.random.uniform(jax.random.fold_in(own, dim), (blocks,), jnp.float32, smallest / len(shards), largest / len(shards)))
        loudness = loudness * jnp.repeat(steps, extent[dim] // blocks).reshape([-1 if axis == dim else 1 for axis in range(len(extent))])
    return loudness


def scatter_about(own_key, extent, scale, limit, split=(), kind=jnp.bfloat16):
    result = jax.random.normal(own_key, extent, jnp.float32) * scale
    if len(split) > 0:
        result = shard_levels(own_key, extent, split, -0.22, 0.18) * result
    return jnp.clip(result, min=-limit, max=limit).astype(kind)


def setup_inputs(seed: int = 0) -> dict:
    streams_of = jax.random.split(jax.random.key(seed), 4)
    orbitals = scatter_about(streams_of[0], (BANDS, GRID, GRID, GRID), 1.0, 6.0, ((0, 16), (1, 16)))
    owner_order = draw_owner_order(jax.random.fold_in(streams_of[3], 71), 0)
    sphere_mask = draw_sphere_mask(jax.random.fold_in(streams_of[3], 71), 0)
    return dict(orbitals=orbitals, owner_order=owner_order, sphere_mask=sphere_mask)


def kernel_table(sphere_mask):
    points = sphere_mask.shape[0]
    grid_index = jnp.arange(points, dtype=jnp.int32)
    signed = jnp.where(grid_index < points // 2, grid_index, grid_index - points)
    square = signed * signed
    total_sq = square[:, None, None] + square[None, :, None] + square[None, None, :]
    inverse = jnp.where(total_sq > 0, 1.0 / jnp.maximum(total_sq, 1).astype(jnp.float32), jnp.float32(0.0))
    return sphere_mask.astype(jnp.float32) * inverse * jnp.float32(1.0 / (3.0 * float(points)))


def settle(values):
    real_part, imag_part = lax.optimization_barrier((jnp.real(values).astype(jnp.bfloat16), jnp.imag(values).astype(jnp.bfloat16)))
    return lax.complex(real_part.astype(jnp.float32), imag_part.astype(jnp.float32))


def potential(dens_re, dens_im, kernel):
    packed = lax.complex(dens_re.astype(jnp.float32), dens_im.astype(jnp.float32))
    section_one = settle(jnp.fft.fft(packed, axis=2))
    section_two = settle(jnp.fft.fft(section_one, axis=1))
    section_three = settle(jnp.fft.fft(section_two, axis=0) * kernel)
    section_four = settle(jnp.fft.ifft(section_three, axis=0, norm="forward"))
    section_five = settle(jnp.fft.ifft(section_four, axis=1, norm="forward"))
    section_six = jnp.fft.ifft(section_five, axis=2, norm="forward")
    return jnp.real(section_six), jnp.imag(section_six)


def reference(orbitals, owner_order, sphere_mask):
    per_group = B_DEV
    kernel = kernel_table(sphere_mask)

    def one_band(local):
        local_values = local.astype(jnp.float32)
        accumulated = jnp.zeros(local.shape, jnp.float32)
        for round_index in range(ROUNDS):
            start = (owner_order[round_index] * per_group).astype(jnp.int32)
            owner_rows = lax.dynamic_slice_in_dim(orbitals, start, per_group, 0)
            for pack in range(per_group // 2):
                first_one = owner_rows[2 * pack].astype(jnp.float32)
                second_one = owner_rows[2 * pack + 1].astype(jnp.float32)
                dens_re = (first_one * local_values).astype(jnp.bfloat16)
                dens_im = (second_one * local_values).astype(jnp.bfloat16)
                pot_real, pot_imag = potential(dens_re, dens_im, kernel)
                accumulated = accumulated - first_one * pot_real - second_one * pot_imag
        return accumulated

    return lax.map(one_band, orbitals)
```

```python
import functools
import math

import jax
import jax.numpy as jnp
import ml_dtypes
import numpy as np
from jax import lax
from jax.experimental import pallas as pl
from jax.experimental.pallas import tpu as pltpu
from jax.sharding import PartitionSpec as P

MESH = pl.DeviceIdType.MESH
N = 128
NZ = 8
NF = 16
F32 = jnp.float32
BF16 = jnp.bfloat16


def dft_tables():
    k = np.arange(N)
    phases = 2.0 * math.pi / N * ((k[:, None] * k[None, :]) % N)
    c, s = np.cos(phases), np.sin(phases)
    forward = np.block([[c, s], [-s, c]])
    inverse = np.block([[c, -s], [s, c]])
    pairs = np.arange(2 * N).reshape(2, N).T.reshape(-1)
    tables = (
        forward.T,
        inverse.T,
        forward,
        inverse,
        forward[:, pairs],
        inverse[pairs, :],
    )
    return np.stack(tables).astype(ml_dtypes.bfloat16)


def body(
    order_ref, orb_ref, mask_ref, tab_ref, out_ref,
    own15, owng, masked, parts, partial, half,
    kern, rows_f32, out_send, out_land, ret_send, ret_land,
    send_sem, land_sem, cast_send, cast_land,
    scatter_send, scatter_land, gather_send, gather_land, cross_send, cross_land, local_sem,
):
    band = lax.axis_index("band")
    f = lax.axis_index("fft")
    z = band // 2
    xh = band % 2

    barrier = pltpu.get_barrier_semaphore()

    def greet(device):
        pl.semaphore_signal(barrier, inc=1, device_id=device, device_id_type=MESH)

    def z_peer(k):
        return (((z + k) % NZ) * 2 + xh, f)

    across = (z * 2 + 1 - xh, f)

    @pl.loop(1, NF)
    def _(k):
        greet((band, (f + k) % NF))

    @pl.loop(1, NZ)
    def _(k):
        greet(z_peer(k))

    greet(across)

    def signed(v):
        return jnp.where(v < N // 2, v, v - N)

    @pl.loop(0, 8)
    def _(k):
        along_z = signed(lax.broadcasted_iota(jnp.int32, (N, N), 0))
        along_x = signed(lax.broadcasted_iota(jnp.int32, (N, N), 1))
        along_y = signed(f * 8 + k)
        total = along_z * along_z + along_x * along_x + along_y * along_y
        inverse = jnp.where(total > 0, 1.0 / jnp.maximum(total, 1).astype(F32), F32(0.0))
        bits = mask_ref[pl.ds(k, N, stride=8), :].astype(F32)
        kern[k] = bits * inverse * F32(1.0 / (3.0 * N))

    other = jnp.minimum(order_ref[0], order_ref[1])

    @pl.loop(0, 8)
    def _(p):
        for o in range(2):
            value = orb_ref[o, p]
            masked[p, o] = jnp.where(other == band, value, jnp.zeros_like(value))

    pl.semaphore_wait(barrier, NF - 1 + NZ - 1 + 1)

    def cast_copy(p, way, device):
        return pltpu.make_async_remote_copy(
            src_ref=own15.at[p], dst_ref=own15.at[p],
            send_sem=cast_send.at[way, p], recv_sem=cast_land.at[p],
            device_id=device, device_id_type=MESH,
        )

    root = (z == NZ - 1) & (xh == 1)
    up = (z == NZ - 1) | (z < 3)
    down = z > 4
    to_up = (((z + 1) % NZ) * 2 + xh, f)
    to_down = (((z + NZ - 1) % NZ) * 2 + xh, f)

    def forward_cast(p):
        @pl.when(up)
        def _():
            cast_copy(p, 0, to_up).start()

        @pl.when(down)
        def _():
            cast_copy(p, 1, to_down).start()

        @pl.when(root)
        def _():
            cast_copy(p, 2, across).start()

    def out_copy(unit, j):
        return pltpu.make_async_remote_copy(
            src_ref=out_send.at[unit, j], dst_ref=out_land.at[unit, f],
            send_sem=send_sem.at[0, unit, j], recv_sem=land_sem.at[0, unit, f],
            device_id=(band, j), device_id_type=MESH,
        )

    def out_wait(unit, j):
        pltpu.make_async_remote_copy(
            src_ref=out_send.at[unit, j], dst_ref=out_land.at[unit, j],
            send_sem=send_sem.at[0, unit, j], recv_sem=land_sem.at[0, unit, j],
            device_id=(band, j), device_id_type=MESH,
        ).wait_recv()

    def ret_copy(unit, j):
        return pltpu.make_async_remote_copy(
            src_ref=ret_send.at[unit, j], dst_ref=ret_land.at[unit, f],
            send_sem=send_sem.at[1, unit, j], recv_sem=land_sem.at[1, unit, f],
            device_id=(band, j), device_id_type=MESH,
        )

    def ret_wait(unit, j):
        pltpu.make_async_remote_copy(
            src_ref=ret_send.at[unit, j], dst_ref=ret_land.at[unit, j],
            send_sem=send_sem.at[1, unit, j], recv_sem=land_sem.at[1, unit, j],
            device_id=(band, j), device_id_type=MESH,
        ).wait_recv()

    def scatter_copy(k):
        t = (z + k) % NZ
        return pltpu.make_async_remote_copy(
            src_ref=masked.at[t], dst_ref=parts.at[k],
            send_sem=scatter_send.at[k], recv_sem=scatter_land.at[k],
            device_id=(t * 2 + xh, f), device_id_type=MESH,
        )

    def cross_copy():
        return pltpu.make_async_remote_copy(
            src_ref=partial, dst_ref=half, send_sem=cross_send, recv_sem=cross_land,
            device_id=across, device_id_type=MESH,
        )

    def gather_copy(k):
        t = (z + k) % NZ
        return pltpu.make_async_remote_copy(
            src_ref=parts.at[0], dst_ref=owng.at[z],
            send_sem=gather_send.at[k], recv_sem=gather_land.at[z],
            device_id=(t * 2 + xh, f), device_id_type=MESH,
        )

    def gather_wait(p):
        pltpu.make_async_remote_copy(
            src_ref=parts.at[0], dst_ref=owng.at[p],
            send_sem=gather_send.at[0], recv_sem=gather_land.at[p],
            device_id=across, device_id_type=MESH,
        ).wait_recv()

    def transform_planes(owner, local, first):
        dens = []
        for i in range(2):
            p = first + i
            mine = orb_ref[local, p]
            dens.append(jnp.concatenate([owner[p, 0] * mine, owner[p, 1] * mine], axis=1))
        one = jnp.dot(jnp.concatenate(dens, axis=0), tab_ref[0], preferred_element_type=F32)
        one = one.astype(BF16)
        right = jnp.concatenate(
            [
                jnp.concatenate([one[:N, :N], one[N:, :N]], axis=1),
                jnp.concatenate([one[:N, N:], one[N:, N:]], axis=1),
            ],
            axis=0,
        )
        two = jnp.dot(tab_ref[2], right, preferred_element_type=F32)
        for i in range(2):
            start = pl.multiple_of((first + i) * 2 * N, 2 * N)
            rows_f32[local, pl.ds(start, 2 * N), :] = two[:, i * N : (i + 1) * N]

    def send_out(unit, local):
        @pl.loop(0, NF)
        def _(k):
            j = (f + k) % NF
            for i in range(8):
                tile = rows_f32[local, pl.ds(j * 8 + i, 16, stride=N), :]
                out_send[unit, j, i] = tile.astype(BF16)

            @pl.when(k > 0)
            def _():
                out_copy(unit, j).start()

            @pl.when(k == 0)
            def _():
                pltpu.make_async_copy(
                    out_send.at[unit, j], out_land.at[unit, j], local_sem.at[0, unit]
                ).start()

    def spectrum(unit):
        pltpu.make_async_copy(
            out_send.at[unit, f], out_land.at[unit, f], local_sem.at[0, unit]
        ).wait()

        @pl.loop(1, NF)
        def _(k):
            out_wait(unit, (f + k) % NF)

        @pl.loop(0, 4)
        def _(pair):
            cols = [out_land[unit, :, pair * 2 + i].reshape(2 * N, N) for i in range(2)]
            three = jnp.dot(
                tab_ref[4], jnp.concatenate(cols, axis=1), preferred_element_type=F32
            )
            weights = jnp.concatenate([kern[pair * 2], kern[pair * 2 + 1]], axis=1)
            weights = jnp.concatenate([weights, weights], axis=0)
            three = (three * weights).astype(BF16)
            four = jnp.dot(tab_ref[5], three, preferred_element_type=F32).astype(BF16)
            for i in range(2):
                ret_send[unit, :, pair * 2 + i] = four[:, i * N : (i + 1) * N].reshape(NF, 16, N)

        pltpu.make_async_copy(
            ret_send.at[unit, f], ret_land.at[unit, f], local_sem.at[1, unit]
        ).start()

        @pl.loop(1, NF)
        def _(k):
            ret_copy(unit, (f + k) % NF).start()

    def images(unit, owner, local, fresh):
        pltpu.make_async_copy(
            ret_send.at[unit, f], ret_land.at[unit, f], local_sem.at[1, unit]
        ).wait()

        @pl.loop(0, NF)
        def _(k):
            j = (f + k) % NF

            @pl.when(k > 0)
            def _():
                ret_wait(unit, j)

            value = ret_land[unit, j].astype(F32).reshape(N, N)
            rows_f32[local, pl.ds(pl.multiple_of(j * N, N), N), :] = value

        @pl.loop(0, 4)
        def _(pair):
            first = pair * 2
            planes = []
            for i in range(2):
                row = (first + i) * 2
                re = rows_f32[local, pl.ds(row, N, stride=16), :].astype(BF16)
                im = rows_f32[local, pl.ds(row + 1, N, stride=16), :].astype(BF16)
                planes.append(jnp.concatenate([re, im], axis=0))
            five = jnp.dot(
                tab_ref[3], jnp.concatenate(planes, axis=1), preferred_element_type=F32
            ).astype(BF16)
            left = jnp.concatenate(
                [
                    jnp.concatenate([five[:N, :N], five[N:, :N]], axis=1),
                    jnp.concatenate([five[:N, N:], five[N:, N:]], axis=1),
                ],
                axis=0,
            )
            six = jnp.dot(left, tab_ref[1], preferred_element_type=F32)
            for i in range(2):
                p = first + i
                pot = six[i * N : (i + 1) * N]
                term = owner[p, 0].astype(F32) * pot[:, :N] + owner[p, 1].astype(F32) * pot[:, N:]
                if fresh:
                    out_ref[local, p] = -term
                else:
                    out_ref[local, p] = out_ref[local, p] - term

    def local_cast(p):
        return pltpu.make_async_copy(orb_ref.at[:, p], own15.at[p], cast_land.at[p])

    @pl.when(root)
    def _():
        @pl.loop(0, 8)
        def _(p):
            local_cast(p).start()

    @pl.loop(0, 4)
    def _(pair):
        for i in range(2):
            p = pair * 2 + i

            @pl.when(root)
            def _():
                local_cast(p).wait()

            @pl.when(jnp.logical_not(root))
            def _():
                cast_copy(p, 0, across).wait_recv()

            forward_cast(p)
        for local in range(2):
            transform_planes(own15, local, pair * 2)

    @pl.loop(1, NZ)
    def _(k):
        scatter_copy(k).start()

    for local in range(2):
        send_out(local, local)
    spectrum(0)

    parts[0] = masked[z]

    @pl.loop(1, NZ)
    def _(k):
        scatter_copy(k).wait_recv()
        parts[0] = parts[0] + parts[k]

    partial[...] = parts[0]
    cross_copy().start()
    spectrum(1)
    cross_copy().wait()
    parts[0] = partial[...] + half[...]
    owng[z] = parts[0]

    @pl.loop(1, NZ)
    def _(k):
        gather_copy(k).start()

    @pl.loop(1, NZ)
    def _(k):
        gather_wait((z + k) % NZ)

    for local in range(2):
        @pl.loop(0, 4)
        def _(pair):
            transform_planes(owng, local, pair * 2)

        send_out(2 + local, local)

    for local in range(2):
        images(local, own15, local, True)
    for local in range(2):
        spectrum(2 + local)
    for local in range(2):
        images(2 + local, owng, local, False)

    @pl.loop(0, 8)
    def _(p):
        @pl.when(up)
        def _():
            cast_copy(p, 0, to_up).wait_send()

        @pl.when(down)
        def _():
            cast_copy(p, 1, to_down).wait_send()

        @pl.when(root)
        def _():
            cast_copy(p, 2, across).wait_send()

    @pl.loop(1, NZ)
    def _(k):
        scatter_copy(k).wait_send()
        gather_copy(k).wait_send()

    @pl.loop(0, 4)
    def _(unit):
        @pl.loop(1, NF)
        def _(k):
            out_copy(unit, (f + k) % NF).wait_send()
            ret_copy(unit, (f + k) % NF).wait_send()


def shards(orbitals, owner_order, sphere_mask):
    tables = jnp.asarray(dft_tables())
    mask_rows = sphere_mask.reshape(N * 8, N)
    vmem = pl.BlockSpec(memory_space=pltpu.VMEM)
    dma = pltpu.SemaphoreType.DMA
    plane = (2, N, N)
    return pl.pallas_call(
        body,
        name="exchange",
        out_shape=jax.ShapeDtypeStruct(orbitals.shape, F32),
        in_specs=[pl.BlockSpec(memory_space=pltpu.SMEM), vmem, vmem, vmem],
        out_specs=vmem,
        scratch_shapes=[
            pltpu.VMEM((8,) + plane, BF16),
            pltpu.VMEM((8,) + plane, BF16),
            pltpu.VMEM((8,) + plane, BF16),
            pltpu.VMEM((NZ,) + plane, BF16),
            pltpu.VMEM(plane, BF16),
            pltpu.VMEM(plane, BF16),
            pltpu.VMEM((8, N, N), F32),
            pltpu.VMEM((2, 16 * N, N), F32),
            pltpu.VMEM((4, NF, 8, 16, N), BF16),
            pltpu.VMEM((4, NF, 8, 16, N), BF16),
            pltpu.VMEM((4, NF, 8, 16, N), BF16),
            pltpu.VMEM((4, NF, 8, 16, N), BF16),
            dma((2, 4, NF)),
            dma((2, 4, NF)),
            dma((3, 8)),
            dma((8,)),
            dma((NZ,)),
            dma((NZ,)),
            dma((NZ,)),
            dma((8,)),
            dma(()),
            dma(()),
            dma((2, 4)),
        ],
        compiler_params=pltpu.CompilerParams(
            collective_id=0, has_side_effects=True, vmem_limit_bytes=60 * 1024 * 1024
        ),
    )(owner_order, orbitals, mask_rows, tables)


def solution(mesh):
    placed = (P("band", "fft", None, None), P(), P(None, "fft", None))
    return jax.shard_map(
        shards, mesh=mesh, in_specs=placed, out_specs=P("band", "fft", None, None), check_vma=False
    )
```

```python
import functools
import math

import jax
import jax.numpy as jnp
import ml_dtypes
import numpy as np
from jax import lax
from jax.experimental import pallas as pl
from jax.experimental.pallas import tpu as pltpu
from jax.sharding import PartitionSpec as P

MESH = pl.DeviceIdType.MESH
N = 128
NZ = 8
NF = 16
F32 = jnp.float32
BF16 = jnp.bfloat16
CUTS = 2
PIECE = N // CUTS
LAG = 2


def dft_tables():
    k = np.arange(N)
    phases = 2.0 * math.pi / N * ((k[:, None] * k[None, :]) % N)
    c, s = np.cos(phases), np.sin(phases)
    forward = np.block([[c, s], [-s, c]])
    inverse = np.block([[c, -s], [s, c]])
    pairs = np.arange(2 * N).reshape(2, N).T.reshape(-1)
    tables = (
        forward.T,
        inverse.T,
        forward,
        inverse,
        forward[:, pairs],
        inverse[pairs, :],
    )
    return np.stack(tables).astype(ml_dtypes.bfloat16)


def body(
    order_ref, orb_ref, mask_ref, tab_ref, out_ref,
    own15, owng, masked, parts, partial, half,
    kern, rows_f32, out_send, out_land, ret_send, ret_land,
    send_sem, land_sem, cast_send, cast_land,
    scatter_send, scatter_land, gather_send, gather_land, cross_send, cross_land, local_sem,
):
    band = lax.axis_index("band")
    f = lax.axis_index("fft")
    z = band // 2
    xh = band % 2

    barrier = pltpu.get_barrier_semaphore()

    def greet(device):
        pl.semaphore_signal(barrier, inc=1, device_id=device, device_id_type=MESH)

    def z_peer(k):
        return (((z + k) % NZ) * 2 + xh, f)

    across = (z * 2 + 1 - xh, f)

    @pl.loop(1, NF)
    def _(k):
        greet((band, (f + k) % NF))

    @pl.loop(1, NZ)
    def _(k):
        greet(z_peer(k))

    greet(across)

    def signed(v):
        return jnp.where(v < N // 2, v, v - N)

    @pl.loop(0, 8)
    def _(k):
        along_z = signed(lax.broadcasted_iota(jnp.int32, (N, N), 0))
        along_x = signed(lax.broadcasted_iota(jnp.int32, (N, N), 1))
        along_y = signed(f * 8 + k)
        total = along_z * along_z + along_x * along_x + along_y * along_y
        inverse = jnp.where(total > 0, 1.0 / jnp.maximum(total, 1).astype(F32), F32(0.0))
        bits = mask_ref[pl.ds(k, N, stride=8), :].astype(F32)
        kern[k] = bits * inverse * F32(1.0 / (3.0 * N))

    other = jnp.minimum(order_ref[0], order_ref[1])

    @pl.loop(0, 8)
    def _(p):
        for o in range(2):
            value = orb_ref[o, p]
            masked[p, o] = jnp.where(other == band, value, jnp.zeros_like(value))

    @pl.when((z == NZ - 1) & (xh == 1))
    def _():
        @pl.loop(0, 8)
        def _(p):
            for o in range(2):
                own15[p, o] = orb_ref[o, p]

    pl.semaphore_wait(barrier, NF - 1 + NZ - 1 + 1)

    root = (z == NZ - 1) & (xh == 1)
    up = (z == NZ - 1) | (z < 3)
    down = z > 4
    to_up = (((z + 1) % NZ) * 2 + xh, f)
    to_down = (((z + NZ - 1) % NZ) * 2 + xh, f)
    shares = (z < NZ - 1) | (xh == 1)

    def piece(q, o):
        return own15.at[q // CUTS, o, pl.ds(pl.multiple_of((q % CUTS) * PIECE, PIECE), PIECE)]

    def cast_copy(q, way, o, lands, device):
        return pltpu.make_async_remote_copy(
            src_ref=piece(q, o), dst_ref=piece(q, o),
            send_sem=cast_send.at[way, q], recv_sem=cast_land.at[lands, q],
            device_id=device, device_id_type=MESH,
        )

    def cast_up(q):
        return cast_copy(q, 0, 1 - xh, 0, to_up)

    def cast_down(q):
        return cast_copy(q, 1, 1 - xh, 0, to_down)

    def cast_share(q):
        return cast_copy(q, 2, 1 - xh, 1, across)

    def cast_first(q):
        return cast_copy(q, 3, xh, 0, across)

    def pass_on(q):
        @pl.when(jnp.logical_not(root))
        def _():
            cast_up(q).wait_recv()

        @pl.when(root)
        def _():
            cast_first(q).start()

        @pl.when(up)
        def _():
            cast_up(q).start()

        @pl.when(down)
        def _():
            cast_down(q).start()

        @pl.when(shares)
        def _():
            cast_share(q).start()

    def shared(q):
        @pl.when(jnp.logical_not(root))
        def _():
            cast_copy(q, 2, xh, 1, across).wait_recv()

    def out_copy(unit, j):
        return pltpu.make_async_remote_copy(
            src_ref=out_send.at[unit, j], dst_ref=out_land.at[unit, f],
            send_sem=send_sem.at[0, unit, j], recv_sem=land_sem.at[0, unit, f],
            device_id=(band, j), device_id_type=MESH,
        )

    def out_wait(unit, j):
        pltpu.make_async_remote_copy(
            src_ref=out_send.at[unit, j], dst_ref=out_land.at[unit, j],
            send_sem=send_sem.at[0, unit, j], recv_sem=land_sem.at[0, unit, j],
            device_id=(band, j), device_id_type=MESH,
        ).wait_recv()

    def ret_copy(unit, j):
        return pltpu.make_async_remote_copy(
            src_ref=ret_send.at[unit, j], dst_ref=ret_land.at[unit, f],
            send_sem=send_sem.at[1, unit, j], recv_sem=land_sem.at[1, unit, f],
            device_id=(band, j), device_id_type=MESH,
        )

    def ret_wait(unit, j):
        pltpu.make_async_remote_copy(
            src_ref=ret_send.at[unit, j], dst_ref=ret_land.at[unit, j],
            send_sem=send_sem.at[1, unit, j], recv_sem=land_sem.at[1, unit, j],
            device_id=(band, j), device_id_type=MESH,
        ).wait_recv()

    def scatter_copy(k):
        t = (z + k) % NZ
        return pltpu.make_async_remote_copy(
            src_ref=masked.at[t], dst_ref=parts.at[k],
            send_sem=scatter_send.at[k], recv_sem=scatter_land.at[k],
            device_id=(t * 2 + xh, f), device_id_type=MESH,
        )

    def cross_copy():
        return pltpu.make_async_remote_copy(
            src_ref=partial, dst_ref=half, send_sem=cross_send, recv_sem=cross_land,
            device_id=across, device_id_type=MESH,
        )

    def gather_copy(k):
        t = (z + k) % NZ
        return pltpu.make_async_remote_copy(
            src_ref=parts.at[0], dst_ref=owng.at[z],
            send_sem=gather_send.at[k], recv_sem=gather_land.at[z],
            device_id=(t * 2 + xh, f), device_id_type=MESH,
        )

    def gather_wait(p):
        pltpu.make_async_remote_copy(
            src_ref=parts.at[0], dst_ref=owng.at[p],
            send_sem=gather_send.at[0], recv_sem=gather_land.at[p],
            device_id=across, device_id_type=MESH,
        ).wait_recv()

    def transform_planes(owner, local, first):
        dens = []
        for i in range(2):
            p = first + i
            mine = orb_ref[local, p]
            dens.append(jnp.concatenate([owner[p, 0] * mine, owner[p, 1] * mine], axis=1))
        one = jnp.dot(jnp.concatenate(dens, axis=0), tab_ref[0], preferred_element_type=F32)
        one = one.astype(BF16)
        right = jnp.concatenate(
            [
                jnp.concatenate([one[:N, :N], one[N:, :N]], axis=1),
                jnp.concatenate([one[:N, N:], one[N:, N:]], axis=1),
            ],
            axis=0,
        )
        two = jnp.dot(tab_ref[2], right, preferred_element_type=F32)
        for i in range(2):
            start = pl.multiple_of((first + i) * 2 * N, 2 * N)
            rows_f32[local, pl.ds(start, 2 * N), :] = two[:, i * N : (i + 1) * N]

    def send_out(unit, local):
        @pl.loop(0, NF)
        def _(k):
            j = (f + k) % NF
            for i in range(8):
                tile = rows_f32[local, pl.ds(j * 8 + i, 16, stride=N), :]
                out_send[unit, j, i] = tile.astype(BF16)

            @pl.when(k > 0)
            def _():
                out_copy(unit, j).start()

            @pl.when(k == 0)
            def _():
                pltpu.make_async_copy(
                    out_send.at[unit, j], out_land.at[unit, j], local_sem.at[0, unit]
                ).start()

    def spectrum(unit):
        pltpu.make_async_copy(
            out_send.at[unit, f], out_land.at[unit, f], local_sem.at[0, unit]
        ).wait()

        @pl.loop(1, NF)
        def _(k):
            out_wait(unit, (f + k) % NF)

        @pl.loop(0, 4)
        def _(pair):
            cols = [out_land[unit, :, pair * 2 + i].reshape(2 * N, N) for i in range(2)]
            three = jnp.dot(
                tab_ref[4], jnp.concatenate(cols, axis=1), preferred_element_type=F32
            )
            weights = jnp.concatenate([kern[pair * 2], kern[pair * 2 + 1]], axis=1)
            weights = jnp.concatenate([weights, weights], axis=0)
            three = (three * weights).astype(BF16)
            four = jnp.dot(tab_ref[5], three, preferred_element_type=F32).astype(BF16)
            for i in range(2):
                ret_send[unit, :, pair * 2 + i] = four[:, i * N : (i + 1) * N].reshape(NF, 16, N)

        pltpu.make_async_copy(
            ret_send.at[unit, f], ret_land.at[unit, f], local_sem.at[1, unit]
        ).start()

        @pl.loop(1, NF)
        def _(k):
            ret_copy(unit, (f + k) % NF).start()

    def images(unit, owner, local, fresh):
        pltpu.make_async_copy(
            ret_send.at[unit, f], ret_land.at[unit, f], local_sem.at[1, unit]
        ).wait()

        @pl.loop(0, NF)
        def _(k):
            j = (f + k) % NF

            @pl.when(k > 0)
            def _():
                ret_wait(unit, j)

            value = ret_land[unit, j].astype(F32).reshape(N, N)
            rows_f32[local, pl.ds(pl.multiple_of(j * N, N), N), :] = value

        @pl.loop(0, 4)
        def _(pair):
            first = pair * 2
            planes = []
            for i in range(2):
                row = (first + i) * 2
                re = rows_f32[local, pl.ds(row, N, stride=16), :].astype(BF16)
                im = rows_f32[local, pl.ds(row + 1, N, stride=16), :].astype(BF16)
                planes.append(jnp.concatenate([re, im], axis=0))
            five = jnp.dot(
                tab_ref[3], jnp.concatenate(planes, axis=1), preferred_element_type=F32
            ).astype(BF16)
            left = jnp.concatenate(
                [
                    jnp.concatenate([five[:N, :N], five[N:, :N]], axis=1),
                    jnp.concatenate([five[:N, N:], five[N:, N:]], axis=1),
                ],
                axis=0,
            )
            six = jnp.dot(left, tab_ref[1], preferred_element_type=F32)
            for i in range(2):
                p = first + i
                pot = six[i * N : (i + 1) * N]
                term = owner[p, 0].astype(F32) * pot[:, :N] + owner[p, 1].astype(F32) * pot[:, N:]
                if fresh:
                    out_ref[local, p] = -term
                else:
                    out_ref[local, p] = out_ref[local, p] - term

    per_pair = 2 * CUTS

    @pl.loop(1, NZ)
    def _(k):
        scatter_copy(k).start()

    @pl.loop(0, 4 + LAG)
    def _(step):
        @pl.when(step < 4)
        def _():
            @pl.loop(0, per_pair)
            def _(i):
                pass_on(step * per_pair + i)

        @pl.when(step >= LAG)
        def _():
            pair = step - LAG

            @pl.loop(0, per_pair)
            def _(i):
                shared(pair * per_pair + i)

            for local in range(2):
                transform_planes(own15, local, pair * 2)

    parts[0] = masked[z]

    @pl.loop(1, NZ)
    def _(k):
        scatter_copy(k).wait_recv()
        parts[0] = parts[0] + parts[k]

    partial[...] = parts[0]
    cross_copy().start()
    for local in range(2):
        send_out(local, local)
    cross_copy().wait()
    parts[0] = partial[...] + half[...]
    owng[z] = parts[0]

    @pl.loop(1, NZ)
    def _(k):
        gather_copy(k).start()

    spectrum(0)
    spectrum(1)

    @pl.loop(1, NZ)
    def _(k):
        gather_wait((z + k) % NZ)

    for local in range(2):
        @pl.loop(0, 4)
        def _(pair):
            transform_planes(owng, local, pair * 2)

        send_out(2 + local, local)

    for local in range(2):
        images(local, own15, local, True)
    for local in range(2):
        spectrum(2 + local)
    for local in range(2):
        images(2 + local, owng, local, False)

    @pl.loop(0, 8 * CUTS)
    def _(q):
        @pl.when(up)
        def _():
            cast_up(q).wait_send()

        @pl.when(down)
        def _():
            cast_down(q).wait_send()

        @pl.when(shares)
        def _():
            cast_share(q).wait_send()

        @pl.when(root)
        def _():
            cast_first(q).wait_send()

    @pl.loop(1, NZ)
    def _(k):
        scatter_copy(k).wait_send()
        gather_copy(k).wait_send()

    @pl.loop(0, 4)
    def _(unit):
        @pl.loop(1, NF)
        def _(k):
            out_copy(unit, (f + k) % NF).wait_send()
            ret_copy(unit, (f + k) % NF).wait_send()


def shards(orbitals, owner_order, sphere_mask):
    tables = jnp.asarray(dft_tables())
    mask_rows = sphere_mask.reshape(N * 8, N)
    vmem = pl.BlockSpec(memory_space=pltpu.VMEM)
    dma = pltpu.SemaphoreType.DMA
    plane = (2, N, N)
    return pl.pallas_call(
        body,
        name="exchange",
        out_shape=jax.ShapeDtypeStruct(orbitals.shape, F32),
        in_specs=[pl.BlockSpec(memory_space=pltpu.SMEM), vmem, vmem, vmem],
        out_specs=vmem,
        scratch_shapes=[
            pltpu.VMEM((8,) + plane, BF16),
            pltpu.VMEM((8,) + plane, BF16),
            pltpu.VMEM((8,) + plane, BF16),
            pltpu.VMEM((NZ,) + plane, BF16),
            pltpu.VMEM(plane, BF16),
            pltpu.VMEM(plane, BF16),
            pltpu.VMEM((8, N, N), F32),
            pltpu.VMEM((2, 16 * N, N), F32),
            pltpu.VMEM((4, NF, 8, 16, N), BF16),
            pltpu.VMEM((4, NF, 8, 16, N), BF16),
            pltpu.VMEM((4, NF, 8, 16, N), BF16),
            pltpu.VMEM((4, NF, 8, 16, N), BF16),
            dma((2, 4, NF)),
            dma((2, 4, NF)),
            dma((4, 8 * CUTS)),
            dma((2, 8 * CUTS)),
            dma((NZ,)),
            dma((NZ,)),
            dma((NZ,)),
            dma((8,)),
            dma(()),
            dma(()),
            dma((2, 4)),
        ],
        compiler_params=pltpu.CompilerParams(
            collective_id=0, has_side_effects=True, vmem_limit_bytes=60 * 1024 * 1024
        ),
    )(owner_order, orbitals, mask_rows, tables)


def solution(mesh):
    placed = (P("band", "fft", None, None), P(), P(None, "fft", None))
    return jax.shard_map(
        shards, mesh=mesh, in_specs=placed, out_specs=P("band", "fft", None, None), check_vma=False
    )
```

```python
import functools
import math

import jax
import jax.numpy as jnp
import ml_dtypes
import numpy as np
from jax import lax
from jax.experimental import pallas as pl
from jax.experimental.pallas import tpu as pltpu
from jax.sharding import PartitionSpec as P

MESH = pl.DeviceIdType.MESH
N = 128
NZ = 8
NF = 16
F32 = jnp.float32
BF16 = jnp.bfloat16
CUTS = 2
PIECE = N // CUTS
LAG = 2
LATE_AT = 3


def dft_tables():
    k = np.arange(N)
    phases = 2.0 * math.pi / N * ((k[:, None] * k[None, :]) % N)
    c, s = np.cos(phases), np.sin(phases)
    forward = np.block([[c, s], [-s, c]])
    inverse = np.block([[c, -s], [s, c]])
    pairs = np.arange(2 * N).reshape(2, N).T.reshape(-1)
    tables = (
        forward.T,
        inverse.T,
        forward,
        inverse,
        inverse[pairs, :],
    )
    z_half = forward.reshape(2 * N, 2, NF, 2, 4).transpose(0, 3, 2, 4, 1)
    wide = np.zeros((2, 2 * N, 2, NF, 2, 4, 2))
    for k in range(2):
        wide[k, :, :, :, k] = z_half
    wide = wide.reshape(4 * N, 4 * N)
    return np.stack(tables).astype(ml_dtypes.bfloat16), wide.astype(ml_dtypes.bfloat16)


def body(
    order_ref, orb_ref, mask_ref, tab_ref, wide_ref, out_ref,
    own15, owng, masked, parts, partial, half,
    kern, rows_f32, out_send, out_land, ret_send, ret_land,
    out_send_sem, out_land_sem, send_sem, land_sem, cast_send, cast_land,
    scatter_send, scatter_land, gather_send, gather_land, cross_send, cross_land, local_sem,
):
    band = lax.axis_index("band")
    f = lax.axis_index("fft")
    z = band // 2
    xh = band % 2

    barrier = pltpu.get_barrier_semaphore()

    def greet(device):
        pl.semaphore_signal(barrier, inc=1, device_id=device, device_id_type=MESH)

    def z_peer(k):
        return (((z + k) % NZ) * 2 + xh, f)

    across = (z * 2 + 1 - xh, f)

    @pl.loop(1, NF)
    def _(k):
        greet((band, (f + k) % NF))

    @pl.loop(1, NZ)
    def _(k):
        greet(z_peer(k))

    greet(across)

    def signed(v):
        return jnp.where(v < N // 2, v, v - N)

    @pl.loop(0, 8)
    def _(k):
        along_z = signed(lax.broadcasted_iota(jnp.int32, (N, N), 0))
        along_x = signed(lax.broadcasted_iota(jnp.int32, (N, N), 1))
        along_y = signed(f * 8 + k)
        total = along_z * along_z + along_x * along_x + along_y * along_y
        inverse = jnp.where(total > 0, 1.0 / jnp.maximum(total, 1).astype(F32), F32(0.0))
        bits = mask_ref[pl.ds(k, N, stride=8), :].astype(F32)
        kern[k] = bits * inverse * F32(1.0 / (3.0 * N))

    other = jnp.minimum(order_ref[0], order_ref[1])

    @pl.loop(0, 8)
    def _(p):
        for o in range(2):
            value = orb_ref[o, p]
            masked[p, o] = jnp.where(other == band, value, jnp.zeros_like(value))

    @pl.when((z == NZ - 1) & (xh == 1))
    def _():
        @pl.loop(0, 8)
        def _(p):
            for o in range(2):
                own15[p, o] = orb_ref[o, p]

    pl.semaphore_wait(barrier, NF - 1 + NZ - 1 + 1)

    root = (z == NZ - 1) & (xh == 1)
    up = (z == NZ - 1) | (z < 2)
    down = z > 3
    to_up = (((z + 1) % NZ) * 2 + xh, f)
    to_down = (((z + NZ - 1) % NZ) * 2 + xh, f)
    shares = (z < NZ - 1) | (xh == 1)

    def piece(q, o):
        return own15.at[q // CUTS, o, pl.ds(pl.multiple_of((q % CUTS) * PIECE, PIECE), PIECE)]

    def cast_copy(q, way, o, lands, device):
        return pltpu.make_async_remote_copy(
            src_ref=piece(q, o), dst_ref=piece(q, o),
            send_sem=cast_send.at[way], recv_sem=cast_land.at[lands, q],
            device_id=device, device_id_type=MESH,
        )

    def cast_up(q):
        return cast_copy(q, 0, 1 - xh, 0, to_up)

    def cast_down(q):
        return cast_copy(q, 1, 1 - xh, 0, to_down)

    def cast_share(q):
        return cast_copy(q, 2, 1 - xh, 1, across)

    def cast_first(q):
        return cast_copy(q, 3, xh, 0, across)

    def pass_on(q):
        @pl.when(jnp.logical_not(root))
        def _():
            cast_up(q).wait_recv()

        @pl.when(up)
        def _():
            cast_up(q).start()

        @pl.when(down)
        def _():
            cast_down(q).start()

        @pl.when(shares)
        def _():
            cast_share(q).start()

    def shared(q):
        @pl.when(jnp.logical_not(root))
        def _():
            cast_copy(q, 2, xh, 1, across).wait_recv()

    def out_copy(unit, c, j):
        return pltpu.make_async_remote_copy(
            src_ref=out_send.at[unit, c, j], dst_ref=out_land.at[unit, c, f],
            send_sem=out_send_sem.at[unit, c], recv_sem=out_land_sem.at[unit, c],
            device_id=(band, j), device_id_type=MESH,
        )

    def out_all(unit, c):
        rest = pl.ds(0, NF - 1)
        return pltpu.make_async_remote_copy(
            src_ref=out_send.at[unit, c, rest], dst_ref=out_land.at[unit, c, rest],
            send_sem=out_send_sem.at[unit, c], recv_sem=out_land_sem.at[unit, c],
            device_id=across, device_id_type=MESH,
        )

    def ret_all(unit):
        rest = pl.ds(0, NF - 1)
        return pltpu.make_async_remote_copy(
            src_ref=ret_send.at[unit, rest], dst_ref=ret_land.at[unit, rest],
            send_sem=send_sem.at[unit], recv_sem=land_sem.at[unit, 0],
            device_id=across, device_id_type=MESH,
        )

    def ret_copy(unit, j):
        return pltpu.make_async_remote_copy(
            src_ref=ret_send.at[unit, j], dst_ref=ret_land.at[unit, f],
            send_sem=send_sem.at[unit], recv_sem=land_sem.at[unit, f],
            device_id=(band, j), device_id_type=MESH,
        )

    def ret_wait(unit, j):
        pltpu.make_async_remote_copy(
            src_ref=ret_send.at[unit, j], dst_ref=ret_land.at[unit, j],
            send_sem=send_sem.at[unit], recv_sem=land_sem.at[unit, j],
            device_id=(band, j), device_id_type=MESH,
        ).wait_recv()

    def scatter_copy(k):
        t = (z + k) % NZ
        return pltpu.make_async_remote_copy(
            src_ref=masked.at[t], dst_ref=parts.at[k],
            send_sem=scatter_send, recv_sem=scatter_land,
            device_id=(t * 2 + xh, f), device_id_type=MESH,
        )

    def cross_copy():
        return pltpu.make_async_remote_copy(
            src_ref=partial, dst_ref=half, send_sem=cross_send, recv_sem=cross_land,
            device_id=across, device_id_type=MESH,
        )

    def gather_copy(k):
        t = (z + k) % NZ
        return pltpu.make_async_remote_copy(
            src_ref=parts.at[0], dst_ref=owng.at[z],
            send_sem=gather_send, recv_sem=gather_land,
            device_id=(t * 2 + xh, f), device_id_type=MESH,
        )

    def scatter_rest():
        return pltpu.make_async_remote_copy(
            src_ref=masked.at[pl.ds(0, NZ - 1)], dst_ref=parts.at[pl.ds(1, NZ - 1)],
            send_sem=scatter_send, recv_sem=scatter_land,
            device_id=across, device_id_type=MESH,
        )

    def gather_rest():
        rest = pl.ds(0, NZ - 1)
        return pltpu.make_async_remote_copy(
            src_ref=parts.at[rest], dst_ref=owng.at[rest],
            send_sem=gather_send, recv_sem=gather_land,
            device_id=across, device_id_type=MESH,
        )

    def transform_planes(owner, local, first):
        dens = []
        for i in range(2):
            p = first + i
            mine = orb_ref[local, p]
            dens.append(jnp.concatenate([owner[p, 0] * mine, owner[p, 1] * mine], axis=1))
        one = jnp.dot(jnp.concatenate(dens, axis=0), tab_ref[0], preferred_element_type=F32)
        one = one.astype(BF16)
        right = jnp.concatenate(
            [
                jnp.concatenate([one[:N, :N], one[N:, :N]], axis=1),
                jnp.concatenate([one[:N, N:], one[N:, N:]], axis=1),
            ],
            axis=0,
        )
        two = jnp.dot(tab_ref[2], right, preferred_element_type=F32)
        for i in range(2):
            start = pl.multiple_of((first + i) * 2 * N, 2 * N)
            rows_f32[local, pl.ds(start, 2 * N), :] = two[:, i * N : (i + 1) * N]

    def send_out(unit, local, c):
        @pl.loop(0, NF)
        def _(k):
            j = (f + k) % NF
            for i in range(4):
                row = c * 8 * N + j * 8 + i * 2
                tiles = [
                    rows_f32[local, pl.ds(row + ky, 8, stride=N), :] for ky in range(2)
                ]
                out_send[unit, c, j, i] = jnp.concatenate(tiles, axis=0).astype(BF16)

            @pl.when(k > 0)
            def _():
                out_copy(unit, c, j).start()

            @pl.when(k == 0)
            def _():
                pltpu.make_async_copy(
                    out_send.at[unit, c, j], out_land.at[unit, c, j], local_sem.at[c, unit]
                ).start()

    def spectrum(unit):
        for c in range(2):
            pltpu.make_async_copy(
                out_send.at[unit, c, f], out_land.at[unit, c, f], local_sem.at[c, unit]
            ).wait()

            out_all(unit, c).wait_recv()

        @pl.loop(0, 2)
        def _(quad):
            cols = [out_land[unit, :, :, quad * 2 + i].reshape(4 * N, N) for i in range(2)]
            three = jnp.dot(
                wide_ref[...], jnp.concatenate(cols, axis=1), preferred_element_type=F32
            )
            for ky in range(2):
                first = quad * 4 + ky
                weights = jnp.concatenate([kern[first], kern[first + 2]], axis=1)
                weights = jnp.concatenate([weights, weights], axis=0)
                part = (three[ky * 2 * N : (ky + 1) * 2 * N] * weights).astype(BF16)
                four = jnp.dot(tab_ref[4], part, preferred_element_type=F32).astype(BF16)
                for i in range(2):
                    block = four[:, i * N : (i + 1) * N].reshape(NF, 16, N)
                    ret_send[unit, :, first + 2 * i] = block

        pltpu.make_async_copy(
            ret_send.at[unit, f], ret_land.at[unit, f], local_sem.at[2, unit]
        ).start()

        @pl.loop(1, NF)
        def _(k):
            ret_copy(unit, (f + k) % NF).start()

    def images(unit, owner, local, fresh):
        pltpu.make_async_copy(
            ret_send.at[unit, f], ret_land.at[unit, f], local_sem.at[2, unit]
        ).wait()

        @pl.loop(0, NF)
        def _(k):
            j = (f + k) % NF

            @pl.when(k > 0)
            def _():
                ret_wait(unit, j)

            value = ret_land[unit, j].astype(F32).reshape(N, N)
            rows_f32[local, pl.ds(pl.multiple_of(j * N, N), N), :] = value

        @pl.loop(0, 4)
        def _(pair):
            first = pair * 2
            planes = []
            for i in range(2):
                row = (first + i) * 2
                re = rows_f32[local, pl.ds(row, N, stride=16), :].astype(BF16)
                im = rows_f32[local, pl.ds(row + 1, N, stride=16), :].astype(BF16)
                planes.append(jnp.concatenate([re, im], axis=0))
            five = jnp.dot(
                tab_ref[3], jnp.concatenate(planes, axis=1), preferred_element_type=F32
            ).astype(BF16)
            left = jnp.concatenate(
                [
                    jnp.concatenate([five[:N, :N], five[N:, :N]], axis=1),
                    jnp.concatenate([five[:N, N:], five[N:, N:]], axis=1),
                ],
                axis=0,
            )
            six = jnp.dot(left, tab_ref[1], preferred_element_type=F32)
            for i in range(2):
                p = first + i
                pot = six[i * N : (i + 1) * N]
                term = owner[p, 0].astype(F32) * pot[:, :N] + owner[p, 1].astype(F32) * pot[:, N:]
                if fresh:
                    out_ref[local, p] = -term
                else:
                    out_ref[local, p] = out_ref[local, p] - term

    per_pair = 2 * CUTS

    @pl.when(root)
    def _():
        @pl.loop(0, 8 * CUTS)
        def _(q):
            cast_first(q).start()

    def free_route(k):
        return jnp.where(k < 4, (z >= 2) & (z + k <= NZ - 1), (k > 4) & (z <= 3) & (z + k >= NZ - 1))

    @pl.loop(1, NZ)
    def _(k):
        @pl.when(free_route(k))
        def _():
            scatter_copy(k).start()

    @pl.loop(0, 4 + LAG)
    def _(step):
        @pl.when(step < 4)
        def _():
            @pl.loop(0, per_pair)
            def _(i):
                pass_on(step * per_pair + i)

        @pl.when(step >= LAG)
        def _():
            pair = step - LAG

            @pl.loop(0, per_pair)
            def _(i):
                shared(pair * per_pair + i)

            for local in range(2):
                transform_planes(own15, local, pair * 2)

            @pl.when(pair % 2 == 1)
            def _():
                for local in range(2):
                    send_out(local, local, pair // 2)

        @pl.when(step == LATE_AT)
        def _():
            @pl.loop(1, NZ)
            def _(k):
                @pl.when(jnp.logical_not(free_route(k)))
                def _():
                    scatter_copy(k).start()

    scatter_rest().wait_recv()
    partial[...] = masked[z]

    @pl.loop(1, NZ)
    def _(k):
        partial[...] = partial[...] + parts[k]

    cross_copy().start()
    cross_copy().wait()
    parts[0] = partial[...] + half[...]
    owng[z] = parts[0]

    @pl.loop(1, NZ)
    def _(k):
        gather_copy(k).start()

    spectrum(0)
    spectrum(1)

    gather_rest().wait_recv()

    for local in range(2):
        @pl.loop(0, 4)
        def _(pair):
            transform_planes(owng, local, pair * 2)

            @pl.when(pair % 2 == 1)
            def _():
                send_out(2 + local, local, pair // 2)

    for local in range(2):
        images(local, own15, local, True)
    for local in range(2):
        spectrum(2 + local)
    for local in range(2):
        images(2 + local, owng, local, False)

    def cast_left(way, o):
        pltpu.make_async_remote_copy(
            src_ref=own15.at[:, o], dst_ref=own15.at[:, o],
            send_sem=cast_send.at[way], recv_sem=cast_land.at[0, 0],
            device_id=across, device_id_type=MESH,
        ).wait_send()

    @pl.when(up)
    def _():
        cast_left(0, 1 - xh)

    @pl.when(down)
    def _():
        cast_left(1, 1 - xh)

    @pl.when(shares)
    def _():
        cast_left(2, 1 - xh)

    @pl.when(root)
    def _():
        cast_left(3, xh)

    scatter_rest().wait_send()
    gather_rest().wait_send()

    @pl.loop(0, 4)
    def _(unit):
        for c in range(2):
            out_all(unit, c).wait_send()
        ret_all(unit).wait_send()


def shards(orbitals, owner_order, sphere_mask):
    tables, wide = (jnp.asarray(table) for table in dft_tables())
    mask_rows = sphere_mask.reshape(N * 8, N)
    vmem = pl.BlockSpec(memory_space=pltpu.VMEM)
    dma = pltpu.SemaphoreType.DMA
    plane = (2, N, N)
    return pl.pallas_call(
        body,
        name="exchange",
        out_shape=jax.ShapeDtypeStruct(orbitals.shape, F32),
        in_specs=[pl.BlockSpec(memory_space=pltpu.SMEM)] + [vmem] * 4,
        out_specs=vmem,
        scratch_shapes=[
            pltpu.VMEM((8,) + plane, BF16),
            pltpu.VMEM((8,) + plane, BF16),
            pltpu.VMEM((8,) + plane, BF16),
            pltpu.VMEM((NZ,) + plane, BF16),
            pltpu.VMEM(plane, BF16),
            pltpu.VMEM(plane, BF16),
            pltpu.VMEM((8, N, N), F32),
            pltpu.VMEM((2, 16 * N, N), F32),
            pltpu.VMEM((4, 2, NF, 4, 16, N), BF16),
            pltpu.VMEM((4, 2, NF, 4, 16, N), BF16),
            pltpu.VMEM((4, NF, 8, 16, N), BF16),
            pltpu.VMEM((4, NF, 8, 16, N), BF16),
            dma((4, 2)),
            dma((4, 2)),
            dma((4,)),
            dma((4, NF)),
            dma((4,)),
            dma((2, 8 * CUTS)),
            dma(()),
            dma(()),
            dma(()),
            dma(()),
            dma(()),
            dma(()),
            dma((3, 4)),
        ],
        compiler_params=pltpu.CompilerParams(
            collective_id=0, has_side_effects=True, vmem_limit_bytes=60 * 1024 * 1024
        ),
    )(owner_order, orbitals, mask_rows, tables, wide)


def solution(mesh):
    placed = (P("band", "fft", None, None), P(), P(None, "fft", None))
    return jax.shard_map(
        shards, mesh=mesh, in_specs=placed, out_specs=P("band", "fft", None, None), check_vma=False
    )
```

```python
import functools
import math

import jax
import jax.numpy as jnp
import ml_dtypes
import numpy as np
from jax import lax
from jax.experimental import pallas as pl
from jax.experimental.pallas import tpu as pltpu
from jax.sharding import PartitionSpec as P

MESH = pl.DeviceIdType.MESH
N = 128
NZ = 8
NF = 16
F32 = jnp.float32
BF16 = jnp.bfloat16
CUTS = 2
PIECE = N // CUTS
LAG = 2
LATE_AT = 3


def dft_tables():
    k = np.arange(N)
    phases = 2.0 * math.pi / N * ((k[:, None] * k[None, :]) % N)
    c, s = np.cos(phases), np.sin(phases)
    forward = np.block([[c, s], [-s, c]])
    inverse = np.block([[c, -s], [s, c]])
    pairs = np.arange(2 * N).reshape(2, N).T.reshape(-1)
    tables = (
        forward.T,
        inverse.T,
        forward,
        inverse,
        inverse[pairs, :],
    )
    z_half = forward.reshape(2 * N, 2, NF, 2, 4).transpose(0, 3, 2, 4, 1)
    wide = np.zeros((2, 2 * N, 2, NF, 2, 4, 2))
    for k in range(2):
        wide[k, :, :, :, k] = z_half
    wide = wide.reshape(4 * N, 4 * N)
    return np.stack(tables).astype(ml_dtypes.bfloat16), wide.astype(ml_dtypes.bfloat16)


def body(
    order_ref, orb_ref, mask_ref, tab_ref, wide_ref, out_ref,
    own15, owng, masked, parts, partial, half,
    kern, rows_f32, out_send, out_land, ret_send, ret_land,
    out_send_sem, out_land_sem, send_sem, land_sem, cast_send, cast_land,
    scatter_send, scatter_land, gather_send, gather_land, cross_send, cross_land, local_sem,
):
    band = lax.axis_index("band")
    f = lax.axis_index("fft")
    z = band // 2
    xh = band % 2

    barrier = pltpu.get_barrier_semaphore()

    def greet(device):
        pl.semaphore_signal(barrier, inc=1, device_id=device, device_id_type=MESH)

    def z_peer(k):
        return (((z + k) % NZ) * 2 + xh, f)

    across = (z * 2 + 1 - xh, f)

    @pl.loop(1, NF)
    def _(k):
        greet((band, (f + k) % NF))

    @pl.loop(1, NZ)
    def _(k):
        greet(z_peer(k))

    greet(across)

    def signed(v):
        return jnp.where(v < N // 2, v, v - N)

    @pl.loop(0, 8)
    def _(k):
        along_z = signed(lax.broadcasted_iota(jnp.int32, (N, N), 0))
        along_x = signed(lax.broadcasted_iota(jnp.int32, (N, N), 1))
        along_y = signed(f * 8 + k)
        total = along_z * along_z + along_x * along_x + along_y * along_y
        inverse = jnp.where(total > 0, 1.0 / jnp.maximum(total, 1).astype(F32), F32(0.0))
        bits = mask_ref[pl.ds(k, N, stride=8), :].astype(F32)
        kern[k] = bits * inverse * F32(1.0 / (3.0 * N))

    other = jnp.minimum(order_ref[0], order_ref[1])

    @pl.loop(0, 8)
    def _(p):
        for o in range(2):
            value = orb_ref[o, p]
            masked[p, o] = jnp.where(other == band, value, jnp.zeros_like(value))

    @pl.when((z == NZ - 1) & (xh == 1))
    def _():
        @pl.loop(0, 8)
        def _(p):
            for o in range(2):
                own15[p, o] = orb_ref[o, p]

    pl.semaphore_wait(barrier, NF - 1 + NZ - 1 + 1)

    root = (z == NZ - 1) & (xh == 1)
    up = (z == NZ - 1) | (z < 2)
    down = z > 3
    to_up = (((z + 1) % NZ) * 2 + xh, f)
    to_down = (((z + NZ - 1) % NZ) * 2 + xh, f)
    shares = (z < NZ - 1) | (xh == 1)

    def piece(q, o):
        return own15.at[q // CUTS, o, pl.ds(pl.multiple_of((q % CUTS) * PIECE, PIECE), PIECE)]

    def cast_copy(q, way, o, lands, device):
        return pltpu.make_async_remote_copy(
            src_ref=piece(q, o), dst_ref=piece(q, o),
            send_sem=cast_send.at[way], recv_sem=cast_land.at[lands, q],
            device_id=device, device_id_type=MESH,
        )

    def cast_up(q):
        return cast_copy(q, 0, 1 - xh, 0, to_up)

    def cast_down(q):
        return cast_copy(q, 1, 1 - xh, 0, to_down)

    def cast_share(q):
        return cast_copy(q, 2, 1 - xh, 1, across)

    def cast_first(q):
        return cast_copy(q, 3, xh, 0, across)

    def pass_on(q):
        @pl.when(jnp.logical_not(root))
        def _():
            cast_up(q).wait_recv()

        @pl.when(up)
        def _():
            cast_up(q).start()

        @pl.when(down)
        def _():
            cast_down(q).start()

        @pl.when(shares)
        def _():
            cast_share(q).start()

    def shared(q):
        @pl.when(jnp.logical_not(root))
        def _():
            cast_copy(q, 2, xh, 1, across).wait_recv()

    def out_copy(unit, c, j):
        return pltpu.make_async_remote_copy(
            src_ref=out_send.at[unit, c, j], dst_ref=out_land.at[unit, c, f],
            send_sem=out_send_sem.at[unit, c], recv_sem=out_land_sem.at[unit, c],
            device_id=(band, j), device_id_type=MESH,
        )

    def out_all(unit, c):
        rest = pl.ds(0, NF - 1)
        return pltpu.make_async_remote_copy(
            src_ref=out_send.at[unit, c, rest], dst_ref=out_land.at[unit, c, rest],
            send_sem=out_send_sem.at[unit, c], recv_sem=out_land_sem.at[unit, c],
            device_id=across, device_id_type=MESH,
        )

    def ret_all(unit):
        rest = pl.ds(0, NF - 1)
        return pltpu.make_async_remote_copy(
            src_ref=ret_send.at[unit, rest], dst_ref=ret_land.at[unit, rest],
            send_sem=send_sem.at[unit], recv_sem=land_sem.at[unit],
            device_id=across, device_id_type=MESH,
        )

    def ret_copy(unit, j):
        return pltpu.make_async_remote_copy(
            src_ref=ret_send.at[unit, j], dst_ref=ret_land.at[unit, f],
            send_sem=send_sem.at[unit], recv_sem=land_sem.at[unit],
            device_id=(band, j), device_id_type=MESH,
        )

    def scatter_copy(k):
        t = (z + k) % NZ
        return pltpu.make_async_remote_copy(
            src_ref=masked.at[t], dst_ref=parts.at[k],
            send_sem=scatter_send, recv_sem=scatter_land,
            device_id=(t * 2 + xh, f), device_id_type=MESH,
        )

    def cross_copy():
        return pltpu.make_async_remote_copy(
            src_ref=partial, dst_ref=half, send_sem=cross_send, recv_sem=cross_land,
            device_id=across, device_id_type=MESH,
        )

    def gather_copy(k):
        t = (z + k) % NZ
        return pltpu.make_async_remote_copy(
            src_ref=parts.at[0], dst_ref=owng.at[z],
            send_sem=gather_send, recv_sem=gather_land,
            device_id=(t * 2 + xh, f), device_id_type=MESH,
        )

    def scatter_rest():
        return pltpu.make_async_remote_copy(
            src_ref=masked.at[pl.ds(0, NZ - 1)], dst_ref=parts.at[pl.ds(1, NZ - 1)],
            send_sem=scatter_send, recv_sem=scatter_land,
            device_id=across, device_id_type=MESH,
        )

    def gather_rest():
        rest = pl.ds(0, NZ - 1)
        return pltpu.make_async_remote_copy(
            src_ref=parts.at[rest], dst_ref=owng.at[rest],
            send_sem=gather_send, recv_sem=gather_land,
            device_id=across, device_id_type=MESH,
        )

    def transform_planes(owner, local, first):
        dens = []
        for i in range(2):
            p = first + i
            mine = orb_ref[local, p]
            dens.append(jnp.concatenate([owner[p, 0] * mine, owner[p, 1] * mine], axis=1))
        one = jnp.dot(jnp.concatenate(dens, axis=0), tab_ref[0], preferred_element_type=F32)
        one = one.astype(BF16)
        right = jnp.concatenate(
            [
                jnp.concatenate([one[:N, :N], one[N:, :N]], axis=1),
                jnp.concatenate([one[:N, N:], one[N:, N:]], axis=1),
            ],
            axis=0,
        )
        two = jnp.dot(tab_ref[2], right, preferred_element_type=F32)
        for i in range(2):
            start = pl.multiple_of((first + i) * 2 * N, 2 * N)
            rows_f32[local, pl.ds(start, 2 * N), :] = two[:, i * N : (i + 1) * N]

    def send_out(unit, local, c):
        @pl.loop(0, NF)
        def _(k):
            j = (f + k) % NF
            for i in range(4):
                row = c * 8 * N + j * 8 + i * 2
                tiles = [
                    rows_f32[local, pl.ds(row + ky, 8, stride=N), :] for ky in range(2)
                ]
                out_send[unit, c, j, i] = jnp.concatenate(tiles, axis=0).astype(BF16)

            @pl.when(k > 0)
            def _():
                out_copy(unit, c, j).start()

            @pl.when(k == 0)
            def _():
                pltpu.make_async_copy(
                    out_send.at[unit, c, j], out_land.at[unit, c, j], local_sem.at[c, unit]
                ).start()

    def spectrum(unit):
        for c in range(2):
            pltpu.make_async_copy(
                out_send.at[unit, c, f], out_land.at[unit, c, f], local_sem.at[c, unit]
            ).wait()

            out_all(unit, c).wait_recv()

        @pl.loop(0, 2)
        def _(quad):
            cols = [out_land[unit, :, :, quad * 2 + i].reshape(4 * N, N) for i in range(2)]
            three = jnp.dot(
                wide_ref[...], jnp.concatenate(cols, axis=1), preferred_element_type=F32
            )
            for ky in range(2):
                first = quad * 4 + ky
                weights = jnp.concatenate([kern[first], kern[first + 2]], axis=1)
                weights = jnp.concatenate([weights, weights], axis=0)
                part = (three[ky * 2 * N : (ky + 1) * 2 * N] * weights).astype(BF16)
                four = jnp.dot(tab_ref[4], part, preferred_element_type=F32).astype(BF16)
                for i in range(2):
                    block = four[:, i * N : (i + 1) * N].reshape(NF, 16, N)
                    ret_send[unit, :, first + 2 * i] = block

        pltpu.make_async_copy(
            ret_send.at[unit, f], ret_land.at[unit, f], local_sem.at[2, unit]
        ).start()

        for k in range(1, NF):
            ret_copy(unit, (f + k) % NF).start()

    def images(unit, owner, local, fresh):
        pltpu.make_async_copy(
            ret_send.at[unit, f], ret_land.at[unit, f], local_sem.at[2, unit]
        ).wait()

        ret_all(unit).wait_recv()

        @pl.loop(0, NF)
        def _(j):
            value = ret_land[unit, j].astype(F32).reshape(N, N)
            rows_f32[local, pl.ds(pl.multiple_of(j * N, N), N), :] = value

        @pl.loop(0, 4)
        def _(pair):
            first = pair * 2
            planes = []
            for i in range(2):
                row = (first + i) * 2
                re = rows_f32[local, pl.ds(row, N, stride=16), :].astype(BF16)
                im = rows_f32[local, pl.ds(row + 1, N, stride=16), :].astype(BF16)
                planes.append(jnp.concatenate([re, im], axis=0))
            five = jnp.dot(
                tab_ref[3], jnp.concatenate(planes, axis=1), preferred_element_type=F32
            ).astype(BF16)
            left = jnp.concatenate(
                [
                    jnp.concatenate([five[:N, :N], five[N:, :N]], axis=1),
                    jnp.concatenate([five[:N, N:], five[N:, N:]], axis=1),
                ],
                axis=0,
            )
            six = jnp.dot(left, tab_ref[1], preferred_element_type=F32)
            for i in range(2):
                p = first + i
                pot = six[i * N : (i + 1) * N]
                term = owner[p, 0].astype(F32) * pot[:, :N] + owner[p, 1].astype(F32) * pot[:, N:]
                if fresh:
                    out_ref[local, p] = -term
                else:
                    out_ref[local, p] = out_ref[local, p] - term

    per_pair = 2 * CUTS

    @pl.when(root)
    def _():
        @pl.loop(0, 8 * CUTS)
        def _(q):
            cast_first(q).start()

    def free_route(k):
        return jnp.where(k < 4, (z >= 2) & (z + k <= NZ - 1), (k > 4) & (z <= 3) & (z + k >= NZ - 1))

    @pl.loop(1, NZ)
    def _(k):
        @pl.when(free_route(k))
        def _():
            scatter_copy(k).start()

    @pl.loop(0, 4 + LAG)
    def _(step):
        @pl.when(step < 4)
        def _():
            @pl.loop(0, per_pair)
            def _(i):
                pass_on(step * per_pair + i)

        @pl.when(step >= LAG)
        def _():
            pair = step - LAG

            @pl.loop(0, per_pair)
            def _(i):
                shared(pair * per_pair + i)

            for local in range(2):
                transform_planes(own15, local, pair * 2)

            @pl.when(pair % 2 == 1)
            def _():
                for local in range(2):
                    send_out(local, local, pair // 2)

        @pl.when(step == LATE_AT)
        def _():
            @pl.loop(1, NZ)
            def _(k):
                @pl.when(jnp.logical_not(free_route(k)))
                def _():
                    scatter_copy(k).start()

    scatter_rest().wait_recv()
    partial[...] = masked[z]

    @pl.loop(1, NZ)
    def _(k):
        partial[...] = partial[...] + parts[k]

    cross_copy().start()
    cross_copy().wait()
    parts[0] = partial[...] + half[...]
    owng[z] = parts[0]

    @pl.loop(1, NZ)
    def _(k):
        gather_copy(k).start()

    spectrum(0)
    spectrum(1)

    gather_rest().wait_recv()

    for local in range(2):
        @pl.loop(0, 4)
        def _(pair):
            transform_planes(owng, local, pair * 2)

            @pl.when(pair % 2 == 1)
            def _():
                send_out(2 + local, local, pair // 2)

    for local in range(2):
        images(local, own15, local, True)
    for local in range(2):
        spectrum(2 + local)
    for local in range(2):
        images(2 + local, owng, local, False)

    def cast_left(way, o):
        pltpu.make_async_remote_copy(
            src_ref=own15.at[:, o], dst_ref=own15.at[:, o],
            send_sem=cast_send.at[way], recv_sem=cast_land.at[0, 0],
            device_id=across, device_id_type=MESH,
        ).wait_send()

    @pl.when(up)
    def _():
        cast_left(0, 1 - xh)

    @pl.when(down)
    def _():
        cast_left(1, 1 - xh)

    @pl.when(shares)
    def _():
        cast_left(2, 1 - xh)

    @pl.when(root)
    def _():
        cast_left(3, xh)

    scatter_rest().wait_send()
    gather_rest().wait_send()

    @pl.loop(0, 4)
    def _(unit):
        for c in range(2):
            out_all(unit, c).wait_send()
        ret_all(unit).wait_send()


def shards(orbitals, owner_order, sphere_mask):
    tables, wide = (jnp.asarray(table) for table in dft_tables())
    mask_rows = sphere_mask.reshape(N * 8, N)
    vmem = pl.BlockSpec(memory_space=pltpu.VMEM)
    dma = pltpu.SemaphoreType.DMA
    plane = (2, N, N)
    return pl.pallas_call(
        body,
        name="exchange",
        out_shape=jax.ShapeDtypeStruct(orbitals.shape, F32),
        in_specs=[pl.BlockSpec(memory_space=pltpu.SMEM)] + [vmem] * 4,
        out_specs=vmem,
        scratch_shapes=[
            pltpu.VMEM((8,) + plane, BF16),
            pltpu.VMEM((8,) + plane, BF16),
            pltpu.VMEM((8,) + plane, BF16),
            pltpu.VMEM((NZ,) + plane, BF16),
            pltpu.VMEM(plane, BF16),
            pltpu.VMEM(plane, BF16),
            pltpu.VMEM((8, N, N), F32),
            pltpu.VMEM((2, 16 * N, N), F32),
            pltpu.VMEM((4, 2, NF, 4, 16, N), BF16),
            pltpu.VMEM((4, 2, NF, 4, 16, N), BF16),
            pltpu.VMEM((4, NF, 8, 16, N), BF16),
            pltpu.VMEM((4, NF, 8, 16, N), BF16),
            dma((4, 2)),
            dma((4, 2)),
            dma((4,)),
            dma((4,)),
            dma((4,)),
            dma((2, 8 * CUTS)),
            dma(()),
            dma(()),
            dma(()),
            dma(()),
            dma(()),
            dma(()),
            dma((3, 4)),
        ],
        compiler_params=pltpu.CompilerParams(
            collective_id=0, has_side_effects=True, vmem_limit_bytes=60 * 1024 * 1024
        ),
    )(owner_order, orbitals, mask_rows, tables, wide)


def solution(mesh):
    placed = (P("band", "fft", None, None), P(), P(None, "fft", None))
    return jax.shard_map(
        shards, mesh=mesh, in_specs=placed, out_specs=P("band", "fft", None, None), check_vma=False
    )
```

```python
import functools
import math

import jax
import jax.numpy as jnp
import ml_dtypes
import numpy as np
from jax import lax
from jax.experimental import pallas as pl
from jax.experimental.pallas import tpu as pltpu
from jax.sharding import PartitionSpec as P

MESH = pl.DeviceIdType.MESH
N = 128
NZ = 8
NF = 16
F32 = jnp.float32
BF16 = jnp.bfloat16
CUTS = 2
PIECE = N // CUTS
LAG = 2
LATE_AT = 3


def dft_tables():
    k = np.arange(N)
    phases = 2.0 * math.pi / N * ((k[:, None] * k[None, :]) % N)
    c, s = np.cos(phases), np.sin(phases)
    forward = np.block([[c, s], [-s, c]])
    inverse = np.block([[c, -s], [s, c]])
    pairs = np.arange(2 * N).reshape(2, N).T.reshape(-1)
    tables = (
        forward.T,
        inverse.T,
        forward,
        inverse,
        inverse[pairs, :],
    )
    z_half = forward.reshape(2 * N, 2, NF, 2, 4).transpose(0, 3, 2, 4, 1)
    wide = np.zeros((2, 2 * N, 2, NF, 2, 4, 2))
    for k in range(2):
        wide[k, :, :, :, k] = z_half
    wide = wide.reshape(4 * N, 4 * N)
    return np.stack(tables).astype(ml_dtypes.bfloat16), wide.astype(ml_dtypes.bfloat16)


def body(
    order_ref, orb_ref, mask_ref, tab_ref, wide_ref, out_ref,
    own15, owng, masked, parts, partial, half,
    kern, rows_f32, out_send, out_land, ret_send, ret_land,
    out_send_sem, out_land_sem, send_sem, land_sem, cast_send, cast_land,
    scatter_send, scatter_land, gather_send, gather_land, cross_send, cross_land, local_sem,
):
    band = lax.axis_index("band")
    f = lax.axis_index("fft")
    z = band // 2
    xh = band % 2

    barrier = pltpu.get_barrier_semaphore()

    def greet(device):
        pl.semaphore_signal(barrier, inc=1, device_id=device, device_id_type=MESH)

    def z_peer(k):
        return (((z + k) % NZ) * 2 + xh, f)

    across = (z * 2 + 1 - xh, f)

    @pl.loop(1, NF)
    def _(k):
        greet((band, (f + k) % NF))

    @pl.loop(1, NZ)
    def _(k):
        greet(z_peer(k))

    greet(across)

    def signed(v):
        return jnp.where(v < N // 2, v, v - N)

    @pl.loop(0, 8)
    def _(k):
        along_z = signed(lax.broadcasted_iota(jnp.int32, (N, N), 0))
        along_x = signed(lax.broadcasted_iota(jnp.int32, (N, N), 1))
        along_y = signed(f * 8 + k)
        total = along_z * along_z + along_x * along_x + along_y * along_y
        inverse = jnp.where(total > 0, 1.0 / jnp.maximum(total, 1).astype(F32), F32(0.0))
        bits = mask_ref[pl.ds(k, N, stride=8), :].astype(F32)
        kern[k] = bits * inverse * F32(1.0 / (3.0 * N))

    other = jnp.minimum(order_ref[0], order_ref[1])

    @pl.loop(0, 8)
    def _(p):
        for o in range(2):
            value = orb_ref[o, p]
            masked[p, o] = jnp.where(other == band, value, jnp.zeros_like(value))

    @pl.when((z == NZ - 1) & (xh == 1))
    def _():
        @pl.loop(0, 8)
        def _(p):
            for o in range(2):
                own15[p, o] = orb_ref[o, p]

    pl.semaphore_wait(barrier, NF - 1 + NZ - 1 + 1)

    root = (z == NZ - 1) & (xh == 1)
    up = (z == NZ - 1) | (z < 2)
    down = z > 3
    to_up = (((z + 1) % NZ) * 2 + xh, f)
    to_down = (((z + NZ - 1) % NZ) * 2 + xh, f)
    shares = (z < NZ - 1) | (xh == 1)

    def piece(q, o):
        return own15.at[q // CUTS, o, pl.ds(pl.multiple_of((q % CUTS) * PIECE, PIECE), PIECE)]

    def cast_copy(q, way, o, lands, device):
        return pltpu.make_async_remote_copy(
            src_ref=piece(q, o), dst_ref=piece(q, o),
            send_sem=cast_send.at[way], recv_sem=cast_land.at[lands, q],
            device_id=device, device_id_type=MESH,
        )

    def cast_up(q):
        return cast_copy(q, 0, 1 - xh, 0, to_up)

    def cast_down(q):
        return cast_copy(q, 1, 1 - xh, 0, to_down)

    def cast_share(q):
        return cast_copy(q, 2, 1 - xh, 1, across)

    def cast_first(q):
        return cast_copy(q, 3, xh, 0, across)

    def pass_on(q):
        @pl.when(jnp.logical_not(root))
        def _():
            cast_up(q).wait_recv()

        @pl.when(up)
        def _():
            cast_up(q).start()

        @pl.when(down)
        def _():
            cast_down(q).start()

        @pl.when(shares)
        def _():
            cast_share(q).start()

    def shared(q):
        @pl.when(jnp.logical_not(root))
        def _():
            cast_copy(q, 2, xh, 1, across).wait_recv()

    def out_copy(unit, c, j):
        return pltpu.make_async_remote_copy(
            src_ref=out_send.at[unit, c, j], dst_ref=out_land.at[unit, c, f],
            send_sem=out_send_sem.at[unit, c], recv_sem=out_land_sem.at[unit, c],
            device_id=(band, j), device_id_type=MESH,
        )

    def out_all(unit, c):
        rest = pl.ds(0, NF - 1)
        return pltpu.make_async_remote_copy(
            src_ref=out_send.at[unit, c, rest], dst_ref=out_land.at[unit, c, rest],
            send_sem=out_send_sem.at[unit, c], recv_sem=out_land_sem.at[unit, c],
            device_id=across, device_id_type=MESH,
        )

    def ret_all(unit):
        rest = pl.ds(0, NF - 1)
        return pltpu.make_async_remote_copy(
            src_ref=ret_send.at[unit, rest], dst_ref=ret_land.at[unit, rest],
            send_sem=send_sem.at[unit], recv_sem=land_sem.at[unit],
            device_id=across, device_id_type=MESH,
        )

    def ret_copy(unit, j):
        return pltpu.make_async_remote_copy(
            src_ref=ret_send.at[unit, j], dst_ref=ret_land.at[unit, f],
            send_sem=send_sem.at[unit], recv_sem=land_sem.at[unit],
            device_id=(band, j), device_id_type=MESH,
        )

    def scatter_copy(k):
        t = (z + k) % NZ
        return pltpu.make_async_remote_copy(
            src_ref=masked.at[t], dst_ref=parts.at[k],
            send_sem=scatter_send, recv_sem=scatter_land,
            device_id=(t * 2 + xh, f), device_id_type=MESH,
        )

    def cross_copy():
        return pltpu.make_async_remote_copy(
            src_ref=partial, dst_ref=half, send_sem=cross_send, recv_sem=cross_land,
            device_id=across, device_id_type=MESH,
        )

    def gather_copy(k):
        t = (z + k) % NZ
        return pltpu.make_async_remote_copy(
            src_ref=parts.at[0], dst_ref=owng.at[z],
            send_sem=gather_send, recv_sem=gather_land,
            device_id=(t * 2 + xh, f), device_id_type=MESH,
        )

    def scatter_rest():
        return pltpu.make_async_remote_copy(
            src_ref=masked.at[pl.ds(0, NZ - 1)], dst_ref=parts.at[pl.ds(1, NZ - 1)],
            send_sem=scatter_send, recv_sem=scatter_land,
            device_id=across, device_id_type=MESH,
        )

    def gather_rest():
        rest = pl.ds(0, NZ - 1)
        return pltpu.make_async_remote_copy(
            src_ref=parts.at[rest], dst_ref=owng.at[rest],
            send_sem=gather_send, recv_sem=gather_land,
            device_id=across, device_id_type=MESH,
        )

    def transform_planes(owner, local, first):
        dens = []
        for i in range(2):
            p = first + i
            mine = orb_ref[local, p]
            dens.append(jnp.concatenate([owner[p, 0] * mine, owner[p, 1] * mine], axis=1))
        one = jnp.dot(jnp.concatenate(dens, axis=0), tab_ref[0], preferred_element_type=F32)
        one = one.astype(BF16)
        right = jnp.concatenate(
            [
                jnp.concatenate([one[:N, :N], one[N:, :N]], axis=1),
                jnp.concatenate([one[:N, N:], one[N:, N:]], axis=1),
            ],
            axis=0,
        )
        two = jnp.dot(tab_ref[2], right, preferred_element_type=F32)
        for i in range(2):
            start = pl.multiple_of((first + i) * 2 * N, 2 * N)
            rows_f32[local, pl.ds(start, 2 * N), :] = two[:, i * N : (i + 1) * N]

    def send_out(unit, local, c):
        @pl.loop(0, NF)
        def _(k):
            j = (f + k) % NF
            for i in range(4):
                row = c * 8 * N + j * 8 + i * 2
                tiles = [
                    rows_f32[local, pl.ds(row + ky, 8, stride=N), :] for ky in range(2)
                ]
                out_send[unit, c, j, i] = jnp.concatenate(tiles, axis=0).astype(BF16)

            @pl.when(k > 0)
            def _():
                out_copy(unit, c, j).start()

            @pl.when(k == 0)
            def _():
                pltpu.make_async_copy(
                    out_send.at[unit, c, j], out_land.at[unit, c, j], local_sem.at[c, unit]
                ).start()

    def spectrum(unit):
        for c in range(2):
            pltpu.make_async_copy(
                out_send.at[unit, c, f], out_land.at[unit, c, f], local_sem.at[c, unit]
            ).wait()

            out_all(unit, c).wait_recv()

        @pl.loop(0, 2)
        def _(quad):
            cols = [out_land[unit, :, :, quad * 2 + i].reshape(4 * N, N) for i in range(2)]
            three = jnp.dot(
                wide_ref[...], jnp.concatenate(cols, axis=1), preferred_element_type=F32
            )
            for ky in range(2):
                first = quad * 4 + ky
                weights = jnp.concatenate([kern[first], kern[first + 2]], axis=1)
                weights = jnp.concatenate([weights, weights], axis=0)
                part = (three[ky * 2 * N : (ky + 1) * 2 * N] * weights).astype(BF16)
                four = jnp.dot(tab_ref[4], part, preferred_element_type=F32).astype(BF16)
                for i in range(2):
                    block = four[:, i * N : (i + 1) * N].reshape(NF, 16, N)
                    ret_send[unit, :, first + 2 * i] = block

        pltpu.make_async_copy(
            ret_send.at[unit, f], ret_land.at[unit, f], local_sem.at[2, unit]
        ).start()

        for k in range(1, NF):
            ret_copy(unit, (f + k) % NF).start()

    def images(unit, owner, local, fresh):
        pltpu.make_async_copy(
            ret_send.at[unit, f], ret_land.at[unit, f], local_sem.at[2, unit]
        ).wait()

        ret_all(unit).wait_recv()

        @pl.loop(0, NF)
        def _(j):
            value = ret_land[unit, j].astype(F32).reshape(N, N)
            rows_f32[local, pl.ds(pl.multiple_of(j * N, N), N), :] = value

        @pl.loop(0, 4)
        def _(pair):
            first = pair * 2
            planes = []
            for i in range(2):
                row = (first + i) * 2
                re = rows_f32[local, pl.ds(row, N, stride=16), :].astype(BF16)
                im = rows_f32[local, pl.ds(row + 1, N, stride=16), :].astype(BF16)
                planes.append(jnp.concatenate([re, im], axis=0))
            five = jnp.dot(
                tab_ref[3], jnp.concatenate(planes, axis=1), preferred_element_type=F32
            ).astype(BF16)
            left = jnp.concatenate(
                [
                    jnp.concatenate([five[:N, :N], five[N:, :N]], axis=1),
                    jnp.concatenate([five[:N, N:], five[N:, N:]], axis=1),
                ],
                axis=0,
            )
            six = jnp.dot(left, tab_ref[1], preferred_element_type=F32)
            for i in range(2):
                p = first + i
                pot = six[i * N : (i + 1) * N]
                term = owner[p, 0].astype(F32) * pot[:, :N] + owner[p, 1].astype(F32) * pot[:, N:]
                if fresh:
                    out_ref[local, p] = -term
                else:
                    out_ref[local, p] = out_ref[local, p] - term

    per_pair = 2 * CUTS

    @pl.when(root)
    def _():
        @pl.loop(0, 8 * CUTS)
        def _(q):
            cast_first(q).start()

    def free_route(k):
        return jnp.where(k < 4, (z >= 2) & (z + k <= NZ - 1), (k > 4) & (z <= 3) & (z + k >= NZ - 1))

    @pl.loop(1, NZ)
    def _(k):
        @pl.when(free_route(k))
        def _():
            scatter_copy(k).start()

    @pl.loop(0, 4 + LAG)
    def _(step):
        @pl.when(step < 4)
        def _():
            @pl.loop(0, per_pair)
            def _(i):
                pass_on(step * per_pair + i)

        @pl.when(step >= LAG)
        def _():
            pair = step - LAG

            @pl.loop(0, per_pair)
            def _(i):
                shared(pair * per_pair + i)

            for local in range(2):
                transform_planes(own15, local, pair * 2)

            @pl.when(pair % 2 == 1)
            def _():
                for local in range(2):
                    send_out(local, local, pair // 2)

        @pl.when(step == LATE_AT)
        def _():
            @pl.loop(1, NZ)
            def _(k):
                @pl.when(jnp.logical_not(free_route(k)))
                def _():
                    scatter_copy(k).start()

    scatter_rest().wait_recv()
    partial[...] = masked[z]

    @pl.loop(1, NZ)
    def _(k):
        partial[...] = partial[...] + parts[k]

    cross_copy().start()
    spectrum(0)
    cross_copy().wait()
    parts[0] = partial[...] + half[...]
    owng[z] = parts[0]

    @pl.loop(1, NZ)
    def _(k):
        gather_copy(k).start()

    spectrum(1)

    gather_rest().wait_recv()

    for local in range(2):
        @pl.loop(0, 4)
        def _(pair):
            transform_planes(owng, local, pair * 2)

            @pl.when(pair % 2 == 1)
            def _():
                send_out(2 + local, local, pair // 2)

    for local in range(2):
        images(local, own15, local, True)
    for local in range(2):
        spectrum(2 + local)
    for local in range(2):
        images(2 + local, owng, local, False)

    def cast_left(way, o):
        pltpu.make_async_remote_copy(
            src_ref=own15.at[:, o], dst_ref=own15.at[:, o],
            send_sem=cast_send.at[way], recv_sem=cast_land.at[0, 0],
            device_id=across, device_id_type=MESH,
        ).wait_send()

    @pl.when(up)
    def _():
        cast_left(0, 1 - xh)

    @pl.when(down)
    def _():
        cast_left(1, 1 - xh)

    @pl.when(shares)
    def _():
        cast_left(2, 1 - xh)

    @pl.when(root)
    def _():
        cast_left(3, xh)

    scatter_rest().wait_send()
    gather_rest().wait_send()

    @pl.loop(0, 4)
    def _(unit):
        for c in range(2):
            out_all(unit, c).wait_send()
        ret_all(unit).wait_send()


def shards(orbitals, owner_order, sphere_mask):
    tables, wide = (jnp.asarray(table) for table in dft_tables())
    mask_rows = sphere_mask.reshape(N * 8, N)
    vmem = pl.BlockSpec(memory_space=pltpu.VMEM)
    dma = pltpu.SemaphoreType.DMA
    plane = (2, N, N)
    return pl.pallas_call(
        body,
        name="exchange",
        out_shape=jax.ShapeDtypeStruct(orbitals.shape, F32),
        in_specs=[pl.BlockSpec(memory_space=pltpu.SMEM)] + [vmem] * 4,
        out_specs=vmem,
        scratch_shapes=[
            pltpu.VMEM((8,) + plane, BF16),
            pltpu.VMEM((8,) + plane, BF16),
            pltpu.VMEM((8,) + plane, BF16),
            pltpu.VMEM((NZ,) + plane, BF16),
            pltpu.VMEM(plane, BF16),
            pltpu.VMEM(plane, BF16),
            pltpu.VMEM((8, N, N), F32),
            pltpu.VMEM((2, 16 * N, N), F32),
            pltpu.VMEM((4, 2, NF, 4, 16, N), BF16),
            pltpu.VMEM((4, 2, NF, 4, 16, N), BF16),
            pltpu.VMEM((4, NF, 8, 16, N), BF16),
            pltpu.VMEM((4, NF, 8, 16, N), BF16),
            dma((4, 2)),
            dma((4, 2)),
            dma((4,)),
            dma((4,)),
            dma((4,)),
            dma((2, 8 * CUTS)),
            dma(()),
            dma(()),
            dma(()),
            dma(()),
            dma(()),
            dma(()),
            dma((3, 4)),
        ],
        compiler_params=pltpu.CompilerParams(
            collective_id=0, has_side_effects=True, vmem_limit_bytes=60 * 1024 * 1024
        ),
    )(owner_order, orbitals, mask_rows, tables, wide)


def solution(mesh):
    placed = (P("band", "fft", None, None), P(), P(None, "fft", None))
    return jax.shard_map(
        shards, mesh=mesh, in_specs=placed, out_specs=P("band", "fft", None, None), check_vma=False
    )
```

```python
import functools
import math

import jax
import jax.numpy as jnp
import ml_dtypes
import numpy as np
from jax import lax
from jax.experimental import pallas as pl
from jax.experimental.pallas import tpu as pltpu
from jax.sharding import PartitionSpec as P

MESH = pl.DeviceIdType.MESH
N = 128
NZ = 8
NF = 16
F32 = jnp.float32
BF16 = jnp.bfloat16
CUTS = 2
PIECE = N // CUTS
LAG = 2
LATE_AT = 3


def dft_tables():
    k = np.arange(N)
    phases = 2.0 * math.pi / N * ((k[:, None] * k[None, :]) % N)
    c, s = np.cos(phases), np.sin(phases)
    forward = np.block([[c, s], [-s, c]])
    inverse = np.block([[c, -s], [s, c]])
    pairs = np.arange(2 * N).reshape(2, N).T.reshape(-1)
    tables = (
        forward.T,
        inverse.T,
        forward,
        inverse,
        inverse[pairs, :],
    )
    z_half = forward.reshape(2 * N, 2, NF, 2, 4).transpose(0, 3, 2, 4, 1)
    wide = np.zeros((2, 2 * N, 2, NF, 2, 4, 2))
    for k in range(2):
        wide[k, :, :, :, k] = z_half
    wide = wide.reshape(4 * N, 4 * N)
    return np.stack(tables).astype(ml_dtypes.bfloat16), wide.astype(ml_dtypes.bfloat16)


def body(
    order_ref, orb_ref, mask_ref, tab_ref, wide_ref, out_ref,
    own15, owng, masked, parts, partial, half,
    kern, rows_f32, out_send, out_land, ret_send, ret_land,
    out_send_sem, out_land_sem, send_sem, land_sem, cast_send, cast_land,
    scatter_send, scatter_land, gather_send, gather_land, cross_send, cross_land, local_sem,
):
    band = lax.axis_index("band")
    f = lax.axis_index("fft")
    z = band // 2
    xh = band % 2

    barrier = pltpu.get_barrier_semaphore()

    def greet(device):
        pl.semaphore_signal(barrier, inc=1, device_id=device, device_id_type=MESH)

    def z_peer(k):
        return (((z + k) % NZ) * 2 + xh, f)

    across = (z * 2 + 1 - xh, f)

    @pl.loop(1, NF)
    def _(k):
        greet((band, (f + k) % NF))

    @pl.loop(1, NZ)
    def _(k):
        greet(z_peer(k))

    greet(across)

    def signed(v):
        return jnp.where(v < N // 2, v, v - N)

    @pl.loop(0, 8)
    def _(k):
        along_z = signed(lax.broadcasted_iota(jnp.int32, (N, N), 0))
        along_x = signed(lax.broadcasted_iota(jnp.int32, (N, N), 1))
        along_y = signed(f * 8 + k)
        total = along_z * along_z + along_x * along_x + along_y * along_y
        inverse = jnp.where(total > 0, 1.0 / jnp.maximum(total, 1).astype(F32), F32(0.0))
        bits = mask_ref[pl.ds(k, N, stride=8), :].astype(F32)
        kern[k] = bits * inverse * F32(1.0 / (3.0 * N))

    other = jnp.minimum(order_ref[0], order_ref[1])

    @pl.loop(0, 8)
    def _(p):
        for o in range(2):
            value = orb_ref[o, p]
            masked[p, o] = jnp.where(other == band, value, jnp.zeros_like(value))

    @pl.when((z == NZ - 1) & (xh == 1))
    def _():
        @pl.loop(0, 8)
        def _(p):
            for o in range(2):
                own15[p, o] = orb_ref[o, p]

    pl.semaphore_wait(barrier, NF - 1 + NZ - 1 + 1)

    root = (z == NZ - 1) & (xh == 1)
    up = (z == NZ - 1) | (z < 2)
    down = z > 3
    to_up = (((z + 1) % NZ) * 2 + xh, f)
    to_down = (((z + NZ - 1) % NZ) * 2 + xh, f)
    shares = (z < NZ - 1) | (xh == 1)

    def piece(q, o):
        return own15.at[q // CUTS, o, pl.ds(pl.multiple_of((q % CUTS) * PIECE, PIECE), PIECE)]

    def cast_copy(q, way, o, lands, device):
        return pltpu.make_async_remote_copy(
            src_ref=piece(q, o), dst_ref=piece(q, o),
            send_sem=cast_send.at[way], recv_sem=cast_land.at[lands, q],
            device_id=device, device_id_type=MESH,
        )

    def cast_up(q):
        return cast_copy(q, 0, 1 - xh, 0, to_up)

    def cast_down(q):
        return cast_copy(q, 1, 1 - xh, 0, to_down)

    def cast_share(q):
        return cast_copy(q, 2, 1 - xh, 1, across)

    def cast_first(q):
        return cast_copy(q, 3, xh, 0, across)

    def pass_on(q):
        @pl.when(jnp.logical_not(root))
        def _():
            cast_up(q).wait_recv()

        @pl.when(up)
        def _():
            cast_up(q).start()

        @pl.when(down)
        def _():
            cast_down(q).start()

        @pl.when(shares)
        def _():
            cast_share(q).start()

    def shared(q):
        @pl.when(jnp.logical_not(root))
        def _():
            cast_copy(q, 2, xh, 1, across).wait_recv()

    def out_copy(unit, c, j):
        return pltpu.make_async_remote_copy(
            src_ref=out_send.at[unit, c, j], dst_ref=out_land.at[unit, c, f],
            send_sem=out_send_sem.at[unit, c], recv_sem=out_land_sem.at[unit, c],
            device_id=(band, j), device_id_type=MESH,
        )

    def out_all(unit, c):
        rest = pl.ds(0, NF - 1)
        return pltpu.make_async_remote_copy(
            src_ref=out_send.at[unit, c, rest], dst_ref=out_land.at[unit, c, rest],
            send_sem=out_send_sem.at[unit, c], recv_sem=out_land_sem.at[unit, c],
            device_id=across, device_id_type=MESH,
        )

    def whole_copy(unit, j):
        return pltpu.make_async_remote_copy(
            src_ref=out_send.at[unit, :, j], dst_ref=out_land.at[unit, :, f],
            send_sem=out_send_sem.at[unit, 0], recv_sem=out_land_sem.at[unit, 0],
            device_id=(band, j), device_id_type=MESH,
        )

    def whole_all(unit):
        rest = pl.ds(0, NF - 1)
        return pltpu.make_async_remote_copy(
            src_ref=out_send.at[unit, :, rest], dst_ref=out_land.at[unit, :, rest],
            send_sem=out_send_sem.at[unit, 0], recv_sem=out_land_sem.at[unit, 0],
            device_id=across, device_id_type=MESH,
        )

    def ret_all(unit):
        rest = pl.ds(0, NF - 1)
        return pltpu.make_async_remote_copy(
            src_ref=ret_send.at[unit, rest], dst_ref=ret_land.at[unit, rest],
            send_sem=send_sem.at[unit], recv_sem=land_sem.at[unit],
            device_id=across, device_id_type=MESH,
        )

    def ret_copy(unit, j):
        return pltpu.make_async_remote_copy(
            src_ref=ret_send.at[unit, j], dst_ref=ret_land.at[unit, f],
            send_sem=send_sem.at[unit], recv_sem=land_sem.at[unit],
            device_id=(band, j), device_id_type=MESH,
        )

    def scatter_copy(k):
        t = (z + k) % NZ
        return pltpu.make_async_remote_copy(
            src_ref=masked.at[t], dst_ref=parts.at[k],
            send_sem=scatter_send, recv_sem=scatter_land,
            device_id=(t * 2 + xh, f), device_id_type=MESH,
        )

    def cross_copy():
        return pltpu.make_async_remote_copy(
            src_ref=partial, dst_ref=half, send_sem=cross_send, recv_sem=cross_land,
            device_id=across, device_id_type=MESH,
        )

    def gather_copy(k):
        t = (z + k) % NZ
        return pltpu.make_async_remote_copy(
            src_ref=parts.at[0], dst_ref=owng.at[z],
            send_sem=gather_send, recv_sem=gather_land,
            device_id=(t * 2 + xh, f), device_id_type=MESH,
        )

    def scatter_rest():
        return pltpu.make_async_remote_copy(
            src_ref=masked.at[pl.ds(0, NZ - 1)], dst_ref=parts.at[pl.ds(1, NZ - 1)],
            send_sem=scatter_send, recv_sem=scatter_land,
            device_id=across, device_id_type=MESH,
        )

    def gather_rest():
        rest = pl.ds(0, NZ - 1)
        return pltpu.make_async_remote_copy(
            src_ref=parts.at[rest], dst_ref=owng.at[rest],
            send_sem=gather_send, recv_sem=gather_land,
            device_id=across, device_id_type=MESH,
        )

    def transform_planes(owner, local, first):
        dens = []
        for i in range(2):
            p = first + i
            mine = orb_ref[local, p]
            dens.append(jnp.concatenate([owner[p, 0] * mine, owner[p, 1] * mine], axis=1))
        one = jnp.dot(jnp.concatenate(dens, axis=0), tab_ref[0], preferred_element_type=F32)
        one = one.astype(BF16)
        right = jnp.concatenate(
            [
                jnp.concatenate([one[:N, :N], one[N:, :N]], axis=1),
                jnp.concatenate([one[:N, N:], one[N:, N:]], axis=1),
            ],
            axis=0,
        )
        two = jnp.dot(tab_ref[2], right, preferred_element_type=F32)
        for i in range(2):
            start = pl.multiple_of((first + i) * 2 * N, 2 * N)
            rows_f32[local, pl.ds(start, 2 * N), :] = two[:, i * N : (i + 1) * N]

    def send_out(unit, local, c):
        @pl.loop(0, NF)
        def _(k):
            j = (f + k) % NF
            for i in range(4):
                row = c * 8 * N + j * 8 + i * 2
                tiles = [
                    rows_f32[local, pl.ds(row + ky, 8, stride=N), :] for ky in range(2)
                ]
                out_send[unit, c, j, i] = jnp.concatenate(tiles, axis=0).astype(BF16)

            @pl.when(k > 0)
            def _():
                out_copy(unit, c, j).start()

            @pl.when(k == 0)
            def _():
                pltpu.make_async_copy(
                    out_send.at[unit, c, j], out_land.at[unit, c, j], local_sem.at[c, unit]
                ).start()

    def send_whole(unit, local):
        @pl.loop(0, NF)
        def _(k):
            j = (f + k) % NF
            for c in range(2):
                for i in range(4):
                    row = c * 8 * N + j * 8 + i * 2
                    tiles = [
                        rows_f32[local, pl.ds(row + ky, 8, stride=N), :] for ky in range(2)
                    ]
                    out_send[unit, c, j, i] = jnp.concatenate(tiles, axis=0).astype(BF16)

            @pl.when(k > 0)
            def _():
                whole_copy(unit, j).start()

            @pl.when(k == 0)
            def _():
                for c in range(2):
                    pltpu.make_async_copy(
                        out_send.at[unit, c, j], out_land.at[unit, c, j], local_sem.at[c, unit]
                    ).start()

    def spectrum(unit):
        if unit >= 2:
            whole_all(unit).wait_recv()
        for c in range(2):
            pltpu.make_async_copy(
                out_send.at[unit, c, f], out_land.at[unit, c, f], local_sem.at[c, unit]
            ).wait()

            if unit < 2:
                out_all(unit, c).wait_recv()

        @pl.loop(0, 2)
        def _(quad):
            cols = [out_land[unit, :, :, quad * 2 + i].reshape(4 * N, N) for i in range(2)]
            three = jnp.dot(
                wide_ref[...], jnp.concatenate(cols, axis=1), preferred_element_type=F32
            )
            for ky in range(2):
                first = quad * 4 + ky
                weights = jnp.concatenate([kern[first], kern[first + 2]], axis=1)
                weights = jnp.concatenate([weights, weights], axis=0)
                part = (three[ky * 2 * N : (ky + 1) * 2 * N] * weights).astype(BF16)
                four = jnp.dot(tab_ref[4], part, preferred_element_type=F32).astype(BF16)
                for i in range(2):
                    block = four[:, i * N : (i + 1) * N].reshape(NF, 16, N)
                    ret_send[unit, :, first + 2 * i] = block

        pltpu.make_async_copy(
            ret_send.at[unit, f], ret_land.at[unit, f], local_sem.at[2, unit]
        ).start()

        for k in range(1, NF):
            ret_copy(unit, (f + k) % NF).start()

    def images(unit, owner, local, fresh):
        pltpu.make_async_copy(
            ret_send.at[unit, f], ret_land.at[unit, f], local_sem.at[2, unit]
        ).wait()

        ret_all(unit).wait_recv()

        @pl.loop(0, NF)
        def _(j):
            value = ret_land[unit, j].astype(F32).reshape(N, N)
            rows_f32[local, pl.ds(pl.multiple_of(j * N, N), N), :] = value

        @pl.loop(0, 4)
        def _(pair):
            first = pair * 2
            planes = []
            for i in range(2):
                row = (first + i) * 2
                re = rows_f32[local, pl.ds(row, N, stride=16), :].astype(BF16)
                im = rows_f32[local, pl.ds(row + 1, N, stride=16), :].astype(BF16)
                planes.append(jnp.concatenate([re, im], axis=0))
            five = jnp.dot(
                tab_ref[3], jnp.concatenate(planes, axis=1), preferred_element_type=F32
            ).astype(BF16)
            left = jnp.concatenate(
                [
                    jnp.concatenate([five[:N, :N], five[N:, :N]], axis=1),
                    jnp.concatenate([five[:N, N:], five[N:, N:]], axis=1),
                ],
                axis=0,
            )
            six = jnp.dot(left, tab_ref[1], preferred_element_type=F32)
            for i in range(2):
                p = first + i
                pot = six[i * N : (i + 1) * N]
                term = owner[p, 0].astype(F32) * pot[:, :N] + owner[p, 1].astype(F32) * pot[:, N:]
                if fresh:
                    out_ref[local, p] = -term
                else:
                    out_ref[local, p] = out_ref[local, p] - term

    per_pair = 2 * CUTS

    @pl.when(root)
    def _():
        @pl.loop(0, 8 * CUTS)
        def _(q):
            cast_first(q).start()

    def free_route(k):
        return jnp.where(k < 4, (z >= 2) & (z + k <= NZ - 1), (k > 4) & (z <= 3) & (z + k >= NZ - 1))

    @pl.loop(1, NZ)
    def _(k):
        @pl.when(free_route(k))
        def _():
            scatter_copy(k).start()

    @pl.loop(0, 4 + LAG)
    def _(step):
        @pl.when(step < 4)
        def _():
            @pl.loop(0, per_pair)
            def _(i):
                pass_on(step * per_pair + i)

        @pl.when(step >= LAG)
        def _():
            pair = step - LAG

            @pl.loop(0, per_pair)
            def _(i):
                shared(pair * per_pair + i)

            for local in range(2):
                transform_planes(own15, local, pair * 2)

            @pl.when(pair % 2 == 1)
            def _():
                for local in range(2):
                    send_out(local, local, pair // 2)

        @pl.when(step == LATE_AT)
        def _():
            @pl.loop(1, NZ)
            def _(k):
                @pl.when(jnp.logical_not(free_route(k)))
                def _():
                    scatter_copy(k).start()

    scatter_rest().wait_recv()
    partial[...] = masked[z]

    @pl.loop(1, NZ)
    def _(k):
        partial[...] = partial[...] + parts[k]

    cross_copy().start()
    spectrum(0)
    cross_copy().wait()
    parts[0] = partial[...] + half[...]
    owng[z] = parts[0]

    @pl.loop(1, NZ)
    def _(k):
        gather_copy(k).start()

    spectrum(1)

    gather_rest().wait_recv()

    for local in range(2):
        @pl.loop(0, 4)
        def _(pair):
            transform_planes(owng, local, pair * 2)

        send_whole(2 + local, local)

    for local in range(2):
        images(local, own15, local, True)
    for local in range(2):
        spectrum(2 + local)
    for local in range(2):
        images(2 + local, owng, local, False)

    def cast_left(way, o):
        pltpu.make_async_remote_copy(
            src_ref=own15.at[:, o], dst_ref=own15.at[:, o],
            send_sem=cast_send.at[way], recv_sem=cast_land.at[0, 0],
            device_id=across, device_id_type=MESH,
        ).wait_send()

    @pl.when(up)
    def _():
        cast_left(0, 1 - xh)

    @pl.when(down)
    def _():
        cast_left(1, 1 - xh)

    @pl.when(shares)
    def _():
        cast_left(2, 1 - xh)

    @pl.when(root)
    def _():
        cast_left(3, xh)

    scatter_rest().wait_send()
    gather_rest().wait_send()

    for unit in range(4):
        if unit < 2:
            for c in range(2):
                out_all(unit, c).wait_send()
        else:
            whole_all(unit).wait_send()
        ret_all(unit).wait_send()


def shards(orbitals, owner_order, sphere_mask):
    tables, wide = (jnp.asarray(table) for table in dft_tables())
    mask_rows = sphere_mask.reshape(N * 8, N)
    vmem = pl.BlockSpec(memory_space=pltpu.VMEM)
    dma = pltpu.SemaphoreType.DMA
    plane = (2, N, N)
    return pl.pallas_call(
        body,
        name="exchange",
        out_shape=jax.ShapeDtypeStruct(orbitals.shape, F32),
        in_specs=[pl.BlockSpec(memory_space=pltpu.SMEM)] + [vmem] * 4,
        out_specs=vmem,
        scratch_shapes=[
            pltpu.VMEM((8,) + plane, BF16),
            pltpu.VMEM((8,) + plane, BF16),
            pltpu.VMEM((8,) + plane, BF16),
            pltpu.VMEM((NZ,) + plane, BF16),
            pltpu.VMEM(plane, BF16),
            pltpu.VMEM(plane, BF16),
            pltpu.VMEM((8, N, N), F32),
            pltpu.VMEM((2, 16 * N, N), F32),
            pltpu.VMEM((4, 2, NF, 4, 16, N), BF16),
            pltpu.VMEM((4, 2, NF, 4, 16, N), BF16),
            pltpu.VMEM((4, NF, 8, 16, N), BF16),
            pltpu.VMEM((4, NF, 8, 16, N), BF16),
            dma((4, 2)),
            dma((4, 2)),
            dma((4,)),
            dma((4,)),
            dma((4,)),
            dma((2, 8 * CUTS)),
            dma(()),
            dma(()),
            dma(()),
            dma(()),
            dma(()),
            dma(()),
            dma((3, 4)),
        ],
        compiler_params=pltpu.CompilerParams(
            collective_id=0, has_side_effects=True, vmem_limit_bytes=60 * 1024 * 1024
        ),
    )(owner_order, orbitals, mask_rows, tables, wide)


def solution(mesh):
    placed = (P("band", "fft", None, None), P(), P(None, "fft", None))
    return jax.shard_map(
        shards, mesh=mesh, in_specs=placed, out_specs=P("band", "fft", None, None), check_vma=False
    )
```
